128 devices in a mesh: grp: 2 (over x_lo), seq: 64 (over z, x_hi, y, core).
Axes of the slice: x: 4 (x_hi: 2, x_lo: 2; x = x_hi * 2 + x_lo), y: 4, z: 4, core: 2. Of those that a mesh axis runs over, the one named last changes fastest.
Arguments:
- feats: bfloat16 [128, 128, 384], P('seq', None, 'grp'), may hold values from -6 to 6
- conv_weight: bfloat16 [3, 128, 128], replicated, may hold values from -0.3125 to 0.3125
- conv_bias: float32 [128], replicated, may hold values from -3 to 3
- latent_projection_weight: bfloat16 [16, 128], replicated, may hold values from -0.75 to 0.75
- noise: bfloat16 [128, 16, 384], P('seq', None, 'grp'), may hold values from -6 to 6
- step_index: int32 [1], replicated, may hold values from 0 to 49
- hist: bfloat16 [512, 64], P('seq'), may hold values from -6 to 6
- hist_level: int32 [512], P('seq'), may hold values from 0 to 2
- hist_count: int32 [64], replicated, may hold values from 1 to 8, 384 in all
- w_in: bfloat16 [64, 3072], replicated, may hold values from -2 to 2
- w_hist: bfloat16 [3, 64, 3072], replicated, may hold values from -0.75 to 0.75
- norm_gain: float32 [3072], replicated, may hold values from 0.5 to 2
- w_query: bfloat16 [3072, 1536], P(None, 'grp'), may hold values from -2 to 2
- w_key: bfloat16 [3072, 1536], P(None, 'grp'), may hold values from -2 to 2
- w_value: bfloat16 [3072, 1536], P(None, 'grp'), may hold values from -0.109375 to 0.109375
- q_gain: float32 [128], replicated, may hold values from 0.5 to 6
- k_gain: float32 [128], replicated, may hold values from 0.5 to 6
- w_out: bfloat16 [1536, 3072], P('grp'), may hold values from -0.5 to 0.5
Outputs:
- attention_out: bfloat16 [12288, 3072], P('seq', 'grp')
The draws below stay inside these ranges and needn't reach their ends.
Inputs may be any that keep to these rules, and one draw needn't show every extreme that they name: hist_count[s] of the 8 history slots of seq index s are live; the largest count is exactly 8.
All inputs are finite; a program needn't handle non-finite values.
Results may differ from the reference program's by a relative error of at most 0.0095.
The reference program's roundings to bfloat16 on the way count: a program that leaves them out, or rounds other values in their place, can miss the bound.
Values may be sent and summed in bfloat16 or wider, within the bound.
A program may use at most 256 MiB of HBM per device.

```python
import math
import jax
import jax.numpy as jnp
import numpy as np
from jax import lax

D = 3072
HD = 128
LAT = 16
HEADS = 12
CV = 128
STEPS = 50
PIXW = 384
HROWS = 8
PATCH = 64
FRAMES = 128
TOKENS = 12288
HIST = 512
N_SEQ = 64


def query_matrix(key):
    base_draw = jax.random.normal(jax.random.fold_in(key, 101), (D, HEADS * HD), jnp.float32)
    return base_draw * D ** (-0.5)


def draw_w_query(key, part):
    return jnp.clip(query_matrix(key), -2.0, 2.0).astype(jnp.bfloat16)


def draw_w_key(key, part):
    fresh_part = jax.random.normal(jax.random.fold_in(key, 102), (D, HEADS * HD), jnp.float32) * D ** (-0.5)
    matrix = fresh_part
    return jnp.clip(matrix, -2.0, 2.0).astype(jnp.bfloat16)


def draw_w_in(key, part):
    matrix = jax.random.normal(jax.random.fold_in(key, 104), (PATCH, D), jnp.float32) * PATCH ** (-0.5)
    return jnp.clip(matrix, -2.0, 2.0).astype(jnp.bfloat16)


def gain_draw(key, salt):
    values = jnp.exp(jax.random.uniform(jax.random.fold_in(key, salt), (HD,), jnp.float32, math.log(0.5), math.log(4.0)))
    return values


def draw_q_gain(key, part):
    return gain_draw(key, 105)


def draw_k_gain(key, part):
    return gain_draw(key, 106)


def touch_ends(entries, stream_key, low, largest):
    longest = entries.shape.index(max(entries.shape))
    spots = []
    for shift in (0, 1):
        where = [jax.random.randint(jax.random.fold_in(stream_key, axis), (), 0, length) for axis, length in enumerate(entries.shape)]
        where[longest] = (where[longest] + shift) % entries.shape[longest]
        spots.append(tuple(where))
    return entries.at[spots[0]].set(low).at[spots[1]].set(largest)


def steps_of(own_key, extent, cuts, low, high):
    def one(position, blocks):
        steps = jax.random.uniform(jax.random.fold_in(jax.random.fold_in(own_key, 6), position), (blocks,), jnp.float32, low / len(cuts), high / len(cuts))
        return jnp.repeat(jnp.exp(steps), extent[position] // blocks).reshape((-1,) + (1,) * (len(extent) - position - 1))

    factor_of = one(*cuts[0])
    for cut in cuts[1:]:
        factor_of = factor_of * one(*cut)
    return factor_of


def length_profile(number_of, total, limit, skew):
    loads = [(1 << 20) // math.isqrt(standing ** skew) + 1 for standing in range(2, number_of + 1)]
    rest, given = total - limit - (number_of - 1), [1] * (number_of - 1)
    while rest > 0:
        movable = [i for i in range(number_of - 1) if given[i] < limit]
        pool, remaining = sum([loads[i] for i in movable]), rest
        for i in movable:
            addition = min(limit - given[i], max(1, remaining * loads[i] // pool), rest)
            given[i] = given[i] + addition
            rest = rest - addition
    return np.array([limit] + given)


def uneven(key, amount, total, reach, slope):
    if amount == 2:
        one = jax.random.randint(key, (), max(1, total - reach), min(reach, total - 1) + 1)
        return jnp.stack([one, total - one])
    tallies = jnp.asarray(length_profile(amount, total, reach, slope), jnp.int32)
    twos = (amount - 1) // 2
    donor, taker = tallies[1:1 + 2 * twos:2], tallies[2:2 + 2 * twos:2]
    slack = jnp.minimum(donor - 1, reach - taker)
    shifted = jax.random.randint(jax.random.fold_in(key, 1), (twos,), 0, 1 << 20) % (slack + 1)
    tallies = tallies.at[1:1 + 2 * twos:2].set(donor - shifted).at[2:2 + 2 * twos:2].set(taker + shifted)
    return tallies[jax.random.permutation(jax.random.fold_in(key, 2), amount)]


def scatter_about(key, shape, scale, limit, pieces=(), kind=jnp.bfloat16):
    level = steps_of(key, shape, pieces, -0.22, 0.18) if pieces else 1.0
    values = jax.random.normal(key, shape, jnp.float32) * scale * level
    return jnp.minimum(jnp.maximum(values, -limit), limit).astype(kind)


def setup_inputs(seed: int = 0) -> dict:
    splits = jax.random.split(jax.random.key(seed), 19)
    feats = scatter_about(splits[0], (FRAMES, CV, PIXW), 1.0, 6.0, ((0, 64), (2, 2)))
    conv_weight = scatter_about(splits[1], (3, CV, CV), (3 * CV) ** -0.5, 0.3125)
    conv_bias = scatter_about(splits[2], (CV,), 0.5, 3.0, (), jnp.float32)
    latent_projection_weight = scatter_about(splits[3], (LAT, CV), (CV // 2) ** -0.5, 0.75)
    noise = scatter_about(splits[4], (FRAMES, LAT, PIXW), 1.0, 6.0, ((0, 64), (2, 2)))
    step_index = jax.random.randint(splits[5], (1,), 0, STEPS).astype(jnp.int32)
    hist = scatter_about(splits[6], (HIST, PATCH), 1.0, 6.0, ((0, 64),))
    hist_level = touch_ends(jax.random.randint(splits[7], (HIST,), 0, 3), jax.random.fold_in(splits[7], 1), 0, 2).astype(jnp.int32)
    hist_count = uneven(splits[8], N_SEQ, N_SEQ * HROWS * 3 // 4, HROWS, 2).astype(jnp.int32)
    w_in = draw_w_in(jax.random.fold_in(splits[18], 71), 0)
    w_hist = scatter_about(splits[10], (3, PATCH, D), PATCH ** -0.5, 0.75)
    norm_gain = jnp.clip(jnp.exp(jax.random.uniform(splits[11], (D,), jnp.float32, math.log(0.5), math.log(2.0))), 0.5, 2.0)
    w_query = draw_w_query(jax.random.fold_in(splits[18], 71), 0)
    w_key = draw_w_key(jax.random.fold_in(splits[18], 71), 0)
    w_value = scatter_about(splits[14], (D, HEADS * HD), D ** -0.5, 0.109375, ((1, 2),))
    q_gain = draw_q_gain(jax.random.fold_in(splits[18], 71), 0)
    k_gain = draw_k_gain(jax.random.fold_in(splits[18], 71), 0)
    w_out = scatter_about(splits[17], (HEADS * HD, D), HD ** -0.5, 0.5, ((0, 2),))
    return {"feats": feats, "conv_weight": conv_weight, "conv_bias": conv_bias, "latent_projection_weight": latent_projection_weight, "noise": noise, "step_index": step_index, "hist": hist, "hist_level": hist_level, "hist_count": hist_count, "w_in": w_in, "w_hist": w_hist, "norm_gain": norm_gain, "w_query": w_query, "w_key": w_key, "w_value": w_value, "q_gain": q_gain, "k_gain": k_gain, "w_out": w_out}


EPSILON = 1e-06

def time_embed(step_index, width):
    half_width = width // 2
    frequency = jnp.exp(-math.log(10000.0) * jnp.arange(half_width, dtype=jnp.float32) / half_width)
    angles = step_index[0].astype(jnp.float32) * frequency
    return jnp.concatenate([jnp.cos(angles), jnp.sin(angles)])

def rms_scale(values, gain):
    return values * lax.rsqrt(lax.optimization_barrier(jnp.mean(values * values, axis=-1, keepdims=True)) + EPSILON) * gain

def encode_video_section(feats, conv_weight, conv_bias, latent_projection_weight, noise, sigma):
    frame_count = feats.shape[0]
    padded = jnp.concatenate([jnp.zeros((2,) + feats.shape[1:], feats.dtype), feats], axis=0)
    total = jnp.zeros(feats.shape, jnp.float32)
    for tap_index in range(3):
        window = padded[2 - tap_index:2 - tap_index + frame_count]
        total = total + jnp.einsum('oc,tcp->top', conv_weight[tap_index].astype(jnp.float32), window.astype(jnp.float32))
    hidden_state = jax.nn.silu(total + conv_bias.astype(jnp.float32)[None, :, None]).astype(jnp.bfloat16)
    latent_input = jnp.einsum('qb,zby->zqy', latent_projection_weight.astype(jnp.float32), hidden_state.astype(jnp.float32))
    noisy = ((1.0 - sigma) * latent_input + sigma * noise.astype(jnp.float32)).astype(jnp.bfloat16)
    channels = noisy.shape[1]
    pixels = noisy.shape[2]
    return noisy.reshape(frame_count, channels, pixels // 4, 4).transpose(0, 2, 1, 3).reshape(frame_count * (pixels // 4), channels * 4)

def reference(feats, conv_weight, conv_bias, latent_projection_weight, noise, step_index, hist, hist_level, hist_count, w_in, w_hist, norm_gain, w_query, w_key, w_value, q_gain, k_gain, w_out):
    sigma = (STEPS - step_index[0].astype(jnp.float32)) / STEPS
    patches = encode_video_section(feats, conv_weight, conv_bias, latent_projection_weight, noise, sigma)
    embed = time_embed(step_index, D)
    gain = norm_gain.astype(jnp.float32)
    tokens = rms_scale(jnp.dot(patches, w_in, preferred_element_type=jnp.float32) + embed, gain).astype(jnp.bfloat16)
    history = jnp.zeros((HIST, D), jnp.float32)
    for level in range(3):
        history = history + jnp.dot(hist, w_hist[level], preferred_element_type=jnp.float32) * (hist_level == level).astype(jnp.float32)[:, None]
    history = rms_scale(history, gain).astype(jnp.bfloat16)
    both_rows = jnp.concatenate([tokens, history], axis=0)
    key_total = TOKENS + HIST
    query = rms_scale(jnp.dot(tokens, w_query, preferred_element_type=jnp.float32).reshape(TOKENS, HEADS, HD), q_gain.astype(jnp.float32)).astype(jnp.bfloat16)
    keys = rms_scale(jnp.dot(both_rows, w_key, preferred_element_type=jnp.float32).reshape(key_total, HEADS, HD), k_gain.astype(jnp.float32)).astype(jnp.bfloat16)
    values = jnp.dot(both_rows, w_value, preferred_element_type=jnp.float32).astype(jnp.bfloat16).reshape(key_total, HEADS, HD)
    slot_index = jnp.arange(HIST, dtype=jnp.int32)
    alive = jnp.concatenate([jnp.ones((TOKENS,), dtype=bool), slot_index % HROWS < jnp.repeat(hist_count, HROWS)])
    scale = 1.0 / math.sqrt(HD)

    def one_head(operands):
        q_head, k_head, v_head = operands
        scores = jnp.dot(q_head, k_head.T, preferred_element_type=jnp.float32) * scale
        scores = jnp.where(alive[None, :], scores, -1e+30)
        row_max = lax.optimization_barrier(jnp.max(scores, axis=1, keepdims=True))
        soft = jnp.where(alive[None, :], jnp.exp(scores - row_max), 0.0)
        row_sum = lax.optimization_barrier(jnp.sum(soft, axis=1, keepdims=True))
        return (jnp.dot(soft.astype(jnp.bfloat16), v_head, preferred_element_type=jnp.float32) / row_sum).astype(jnp.bfloat16)
    heads_out = lax.map(one_head, (query.transpose(1, 0, 2), keys.transpose(1, 0, 2), values.transpose(1, 0, 2)))
    merged = heads_out.transpose(1, 0, 2).reshape(TOKENS, HEADS * HD)
    return jnp.dot(merged, w_out, preferred_element_type=jnp.float32).astype(jnp.bfloat16)
```

```python
import functools
import math

import jax
import jax.numpy as jnp
from jax import lax
from jax.experimental import pallas as pl
from jax.experimental.pallas import tpu as pltpu
from jax.sharding import PartitionSpec as P

STEPS = 50
EPSILON = 1e-06
LOG2E = math.log2(math.e)
MESH = pl.DeviceIdType.MESH
BF = jnp.bfloat16
F32 = jnp.float32
HIGH = lax.Precision.HIGHEST
SPAN = 70.0 * LOG2E
SAFE = 75.0 * LOG2E


def time_embed(step_index, width):
    half_width = width // 2
    frequency = jnp.exp(-math.log(10000.0) * jnp.arange(half_width, dtype=F32) / half_width)
    angles = step_index[0].astype(F32) * frequency
    return jnp.concatenate([jnp.cos(angles), jnp.sin(angles)])


def rms_scale(values, gain):
    return values * lax.rsqrt(jnp.mean(values * values, axis=-1, keepdims=True) + EPSILON) * gain


def split(x):
    hi = x.astype(BF)
    return hi, (x - hi.astype(F32)).astype(BF)


def swap(value):
    return lax.ppermute(value, "grp", [(0, 1), (1, 0)])


def gather_kernel(chips, x_ref, out_ref, send_sem, recv_sem, fsend_sem, frecv_sem, local_sem):
    grp = lax.axis_index("grp")
    seq = lax.axis_index("seq")
    core = seq % 2
    chip = seq // 2
    sibling = chip * 2 + 1 - core

    barrier = pltpu.get_barrier_semaphore()
    pl.semaphore_signal(barrier, inc=1, device_id=(grp, sibling), device_id_type=MESH)

    @pl.loop(1, chips)
    def _(k):
        there = ((chip + k) % chips) * 2 + core
        pl.semaphore_signal(barrier, inc=1, device_id=(grp, there), device_id_type=MESH)

    pl.semaphore_wait(barrier, chips)

    def direct(k):
        there = ((chip + k) % chips) * 2 + core
        return pltpu.make_async_remote_copy(
            src_ref=x_ref, dst_ref=out_ref.at[seq], send_sem=send_sem.at[k], recv_sem=recv_sem.at[k],
            device_id=(grp, there), device_id_type=MESH)

    def forward(k):
        source = ((chip - k + chips) % chips) * 2 + core
        return pltpu.make_async_remote_copy(
            src_ref=out_ref.at[source], dst_ref=out_ref.at[source], send_sem=fsend_sem.at[k], recv_sem=frecv_sem.at[k],
            device_id=(grp, sibling), device_id_type=MESH)

    @pl.loop(1, chips)
    def _(k):
        direct(k).start()

    own = pltpu.make_async_copy(x_ref, out_ref.at[seq], local_sem)
    own.start()
    own.wait()
    forward(0).start()

    @pl.loop(1, chips)
    def _(k):
        direct(k).wait_recv()
        forward(k).start()

    @pl.loop(0, chips)
    def _(k):
        forward(k).wait_recv()
        forward(k).wait_send()

    @pl.loop(1, chips)
    def _(k):
        direct(k).wait_send()


def gather_blocks(x, count, ident):
    chips = count // 2
    return pl.pallas_call(
        functools.partial(gather_kernel, chips),
        out_shape=jax.ShapeDtypeStruct((count,) + x.shape, x.dtype),
        in_specs=[pl.BlockSpec(memory_space=pltpu.VMEM)],
        out_specs=pl.BlockSpec(memory_space=pltpu.VMEM),
        scratch_shapes=[
            pltpu.SemaphoreType.DMA((chips,)),
            pltpu.SemaphoreType.DMA((chips,)),
            pltpu.SemaphoreType.DMA((chips,)),
            pltpu.SemaphoreType.DMA((chips,)),
            pltpu.SemaphoreType.DMA,
        ],
        compiler_params=pltpu.CompilerParams(
            collective_id=ident, has_side_effects=True, vmem_limit_bytes=32 << 20
        ),
    )(x)


def unpack(block, kt_ref, vt_ref, c_ref):
    lane = lax.broadcasted_iota(jnp.int32, (64, 128), 1)
    lane16 = lax.broadcasted_iota(jnp.int32, (16, 128), 1)
    for pair in range(2):
        first, second = block[2 * pair].astype(F32), block[2 * pair + 1].astype(F32)

        def rest(x):
            low = x[64:96]
            return jnp.concatenate([low, pltpu.roll(low, 64, 1)], axis=0)

        tails = jnp.where(lane < 64, rest(first), pltpu.roll(rest(second), 64, 1))
        tail16 = jnp.where(lane16 < 64, first[112:128], pltpu.roll(second[112:128], 64, 1))
        parts = [
            (first[0:64], first[96:112]),
            (tails, tail16),
            (second[0:64], second[96:112]),
        ]
        for tile, (p, c16) in enumerate(parts):
            cols = slice((3 * pair + tile) * 128, (3 * pair + tile + 1) * 128)
            scales = c16[0:8] + c16[8:16]
            c_ref[:, cols] = scales
            pb = p.astype(BF)
            kt_ref[0:64, cols] = pb
            kt_ref[128:192, cols] = pb
            s_row = scales[6:7]
            vt_ref[0:64, cols] = (p * s_row).astype(BF)
            s_hi = c16[6:7]
            s_lo = c16[14:15]
            row = lax.broadcasted_iota(jnp.int32, (16, 128), 0)
            extra = jnp.where(row == 0, s_hi, jnp.where(row == 1, s_lo, jnp.where(row == 2, 1.0, 0.0)))
            vt_ref[64:80, cols] = extra.astype(BF)


NT = (((1,), (1,)), ((), ()))


def attend_kernel(heads, rows, steps, g_ref, q_ref, bound_ref, qhat_ref, kh_ref, vh_ref, hbias_ref, aop_ref,
                  out_ref, kt, vt, cs, acc, m_ref, flag):
    hist_scale = LOG2E / math.sqrt(128.0)
    biggest = jnp.max(bound_ref[...])

    one_row = lax.broadcasted_iota(jnp.int32, (64, kt.shape[1]), 0)
    ones = jnp.where(one_row == 0, 1.0, 0.0).astype(BF)
    kt[64:128, :] = ones
    kt[192:256, :] = ones
    vt[80:128, :] = jnp.zeros((48, vt.shape[1]), BF)
    acc[...] = jnp.zeros_like(acc)
    m_ref[...] = bound_ref[...] - SPAN

    def hist_scores(h):
        s = lax.dot_general(qhat_ref[:, h * 128:(h + 1) * 128], kh_ref[:, h * 128:(h + 1) * 128], NT,
                            preferred_element_type=F32)
        return s * hist_scale + hbias_ref[0:1, :]

    @pl.when(biggest > SAFE)
    def _():
        for h in range(heads):
            sl = slice(h * rows, (h + 1) * rows)
            m_ref[sl, :] = jnp.broadcast_to(jnp.max(hist_scores(h), axis=1, keepdims=True), (rows, 128))

        @pl.loop(0, steps)
        def _(i):
            unpack([g_ref[4 * i + b] for b in range(4)], kt, vt, cs)
            for h in range(heads):
                sl = slice(h * rows, (h + 1) * rows)
                s = jnp.dot(q_ref[sl, :], kt[...], preferred_element_type=F32) * cs[h:h + 1, :]
                m_ref[sl, :] = jnp.maximum(m_ref[sl, :], jnp.max(s, axis=1, keepdims=True))

    @pl.loop(0, steps)
    def _(i):
        unpack([g_ref[4 * i + b] for b in range(4)], kt, vt, cs)

        def scores(h):
            return jnp.dot(q_ref[h * rows:(h + 1) * rows, :], kt[...], preferred_element_type=F32)

        ahead = scores(0)
        for h in range(heads):
            s = ahead
            if h + 1 < heads:
                ahead = scores(h + 1)
            sl = slice(h * rows, (h + 1) * rows)
            w = jnp.exp2(s * cs[h:h + 1, :] - m_ref[sl, 0:1]).astype(BF)
            acc[sl, :] += lax.dot_general(w, vt[...], NT, preferred_element_type=F32)

    for h in range(heads):
        sl = slice(h * rows, (h + 1) * rows)
        w = jnp.exp2(hist_scores(h) - m_ref[sl, 0:1])
        total = jnp.sum(w, axis=1, keepdims=True)
        o = jnp.dot(w.astype(BF), vh_ref[:, h * 128:(h + 1) * 128], preferred_element_type=F32)
        a = acc[sl, :]
        hi = a.astype(BF)
        lo = (a - hi.astype(F32)).astype(BF)
        o = o + jnp.dot(hi, aop_ref[0, :, h * 128:(h + 1) * 128], preferred_element_type=F32)
        o = o + jnp.dot(lo, aop_ref[0, :, h * 128:(h + 1) * 128], preferred_element_type=F32)
        o = o + jnp.dot(hi, aop_ref[1, :, h * 128:(h + 1) * 128], preferred_element_type=F32)
        total = total + a[:, 66:67]
        out_ref[:, h * 128:(h + 1) * 128] = (o / total).astype(BF)


def attend(gathered, qop, bound, qhat, kh, vh, hbias, aop):
    count = gathered.shape[0]
    heads = aop.shape[2] // 128
    rows = qhat.shape[0]
    vm = pl.BlockSpec(memory_space=pltpu.VMEM)
    return pl.pallas_call(
        functools.partial(attend_kernel, heads, rows, count // 4),
        out_shape=jax.ShapeDtypeStruct((rows, heads * 128), BF),
        in_specs=[vm] * 8,
        out_specs=vm,
        scratch_shapes=[
            pltpu.VMEM((256, 768), BF),
            pltpu.VMEM((128, 768), BF),
            pltpu.VMEM((8, 768), F32),
            pltpu.VMEM((heads * rows, 128), F32),
            pltpu.VMEM((heads * rows, 128), F32),
            pltpu.SMEM((1,), F32),
        ],
        compiler_params=pltpu.CompilerParams(vmem_limit_bytes=40 << 20),
    )(gathered, qop, bound, qhat, kh, vh, hbias, aop)


def low_rank_kernel(w_in_ref, gain_ref, embed_ref, hx_ref, wh_ref, gain_all_ref, wk_ref, wv_ref, kg_ref,
                    akc_ref, akg_ref, av_ref, kh_ref, vh_ref, pre, tok, acc_k, acc_v):
    step = pl.program_id(0)
    last = pl.num_programs(0) - 1
    width = pre.shape[1]
    chunk = w_in_ref.shape[1]
    slots = hx_ref.shape[0]

    @pl.when(step == 0)
    def _():
        square = jnp.zeros((slots, 1), F32)
        for j in range(width // chunk):
            cols = slice(j * chunk, (j + 1) * chunk)
            part = jnp.dot(hx_ref[...], wh_ref[:, cols], preferred_element_type=F32)
            pre[:, cols] = part
            square = square + jnp.sum(part * part, axis=1, keepdims=True)
        r = lax.rsqrt(square * (1.0 / width) + EPSILON)
        for j in range(width // chunk):
            cols = slice(j * chunk, (j + 1) * chunk)
            tok[j] = (pre[:, cols] * r * gain_all_ref[:, cols]).astype(BF)
        acc_k[...] = jnp.zeros_like(acc_k)
        acc_v[...] = jnp.zeros_like(acc_v)

    low = w_in_ref[...].astype(F32) * gain_ref[...]
    e = jnp.broadcast_to(embed_ref[...] * gain_ref[...], (16, chunk))
    low_hi = low.astype(BF)
    low_lo = (low - low_hi.astype(F32)).astype(BF)
    e_hi = e.astype(BF)
    e_lo = (e - e_hi.astype(F32)).astype(BF)
    left = jnp.concatenate([low_hi, low_lo, e_hi, e_lo, tok[step]], axis=0)
    acc_k[...] += jnp.dot(left, wk_ref[...], preferred_element_type=F32)
    acc_v[...] += jnp.dot(left, wv_ref[...], preferred_element_type=F32)

    @pl.when(step == last)
    def _():
        def parts(acc):
            a = acc[0:64, :] + acc[64:128, :]
            b = acc[128:144, :] + acc[144:160, :]
            row = lax.broadcasted_iota(jnp.int32, b.shape, 0)
            return a, b, row

        def put(ref, a, b, scale):
            full = jnp.concatenate([a, b, jnp.zeros((48, a.shape[1]), F32)], axis=0) * scale
            hi = full.astype(BF)
            ref[0] = hi
            ref[1] = (full - hi.astype(F32)).astype(BF)

        a, b, row = parts(acc_k)
        b = jnp.where(row == 0, b, 0.0)
        put(akc_ref, a, b, 1.0)
        put(akg_ref, a, b, kg_ref[...])
        a, b, row = parts(acc_v)
        put(av_ref, a, jnp.where(row < 2, b, 0.0), 1.0)
        for h in range(kh_ref.shape[1] // 128):
            cols = slice(h * 128, (h + 1) * 128)
            k = acc_k[160:, cols]
            r = lax.rsqrt(jnp.mean(k * k, axis=1, keepdims=True) + EPSILON)
            kh_ref[:, cols] = (k * r * kg_ref[:, cols]).astype(BF)
        vh_ref[...] = acc_v[160:, :].astype(BF)


def low_rank(w_in, gain, embed, hx, w_hist, w_key, w_value, kg):
    width = w_in.shape[1]
    cols = w_key.shape[1]
    slots = hx.shape[0]
    steps = 6
    chunk = width // steps
    whole = lambda shape: pl.BlockSpec(shape, lambda i: (0,) * len(shape))
    ops = jax.ShapeDtypeStruct((2, 128, cols), BF)
    kv = jax.ShapeDtypeStruct((slots, cols), BF)
    return pl.pallas_call(
        low_rank_kernel,
        out_shape=(ops, ops, ops, kv, kv),
        grid=(steps,),
        in_specs=[
            pl.BlockSpec((64, chunk), lambda i: (0, i)),
            pl.BlockSpec((1, chunk), lambda i: (0, i)),
            pl.BlockSpec((1, chunk), lambda i: (0, i)),
            whole(hx.shape), whole(w_hist.shape), whole((1, width)),
            pl.BlockSpec((chunk, cols), lambda i: (i, 0)),
            pl.BlockSpec((chunk, cols), lambda i: (i, 0)),
            whole((1, cols)),
        ],
        out_specs=(whole(ops.shape), whole(ops.shape), whole(ops.shape), whole(kv.shape), whole(kv.shape)),
        scratch_shapes=[
            pltpu.VMEM((slots, width), F32),
            pltpu.VMEM((steps, slots, chunk), BF),
            pltpu.VMEM((slots + 160, cols), F32),
            pltpu.VMEM((slots + 160, cols), F32),
        ],
        compiler_params=pltpu.CompilerParams(vmem_limit_bytes=48 << 20),
        cost_estimate=pl.CostEstimate(flops=4 * 672 * width * cols, bytes_accessed=12 << 20, transcendentals=0),
    )(w_in, gain, embed, hx, w_hist, gain, w_key, w_value, kg)


def encode_kernel(early_ref, feats_ref, cw_ref, bias_ref, lw_ref, noise_ref, sigma_ref, out_ref):
    grp = lax.axis_index("grp")
    sigma = sigma_ref[0]
    frames, channels, pixels = feats_ref.shape
    window = [early_ref[0], early_ref[1], feats_ref[0], feats_ref[1]]
    pixel = lax.broadcasted_iota(jnp.int32, (pixels, out_ref.shape[1]), 0)
    col = lax.broadcasted_iota(jnp.int32, (pixels, out_ref.shape[1]), 1)
    rows = [jnp.zeros((lw_ref.shape[0], out_ref.shape[1]), F32) for _ in range(4)]
    for t in range(frames):
        total = jnp.zeros((channels, pixels), F32)
        for tap in range(3):
            total = total + jnp.dot(cw_ref[tap], window[2 + t - tap], preferred_element_type=F32)
        total = total + bias_ref[...]
        hidden = (total * (1.0 / (1.0 + jnp.exp(-total)))).astype(BF)
        latent = jnp.dot(lw_ref[...], hidden, preferred_element_type=F32)
        noisy = ((1.0 - sigma) * latent + sigma * noise_ref[t].astype(F32)).astype(BF)
        for i in range(4):
            hit = (pixel % 4 == i) & (col == t * (pixels // 2) + grp * (pixels // 4) + pixel // 4)
            rows[i] = rows[i] + jnp.dot(noisy, jnp.where(hit, 1.0, 0.0).astype(BF), preferred_element_type=F32)
    out_ref[...] = jnp.concatenate(rows, axis=0).astype(BF)


def encode(early, feats, conv_weight, conv_bias, lat_weight, noise, sigma):
    vm = pl.BlockSpec(memory_space=pltpu.VMEM)
    return pl.pallas_call(
        encode_kernel,
        out_shape=jax.ShapeDtypeStruct((4 * lat_weight.shape[0], 256), BF),
        in_specs=[vm] * 6 + [pl.BlockSpec(memory_space=pltpu.SMEM)],
        out_specs=vm,
    )(early, feats, conv_weight, conv_bias, lat_weight, noise, sigma)


def tokens_kernel(mine_ref, other_ref, w_in_ref, embed_ref, gain_ref, akc_ref, tok_ref, pay_ref, x_ref):
    rows, width = tok_ref.shape
    heads = akc_ref.shape[2] // 128
    chunk = 512
    pt = mine_ref[...].astype(F32) + other_ref[...].astype(F32)
    lanes = pt.shape[1]
    row = lax.broadcasted_iota(jnp.int32, (64, lanes), 0)
    tall = jnp.concatenate([pt, jnp.where(row == 0, 1.0, 0.0)], axis=0)
    px = jnp.transpose(tall)[:rows].astype(BF)
    p = px[:, :64]
    square = jnp.zeros((rows, 1), F32)
    square_row = jnp.zeros((8, rows), F32)
    ones = jnp.ones((8, chunk), BF)
    for j in range(width // chunk):
        cols = slice(j * chunk, (j + 1) * chunk)
        x = jnp.dot(p, w_in_ref[:, cols], preferred_element_type=F32) + embed_ref[:, cols]
        x_ref[:, cols] = x
        x2 = x * x
        square = square + jnp.sum(x2, axis=1, keepdims=True)
        hi, lo = split(x2)
        square_row = square_row + lax.dot_general(ones, hi, NT, preferred_element_type=F32)
        square_row = square_row + lax.dot_general(ones, lo, NT, preferred_element_type=F32)
    s = lax.rsqrt(square * (1.0 / width) + EPSILON)
    for j in range(width // chunk):
        cols = slice(j * chunk, (j + 1) * chunk)
        tok_ref[:, cols] = (x_ref[:, cols] * s * gain_ref[:, cols]).astype(BF)
    s_row = lax.rsqrt(square_row * (1.0 / width) + EPSILON)
    y = jnp.dot(px, akc_ref[0], preferred_element_type=F32) + jnp.dot(px, akc_ref[1], preferred_element_type=F32)
    hi, lo = split(y * y)
    r8 = lax.broadcasted_iota(jnp.int32, (8, heads * 128), 0)
    c8 = lax.broadcasted_iota(jnp.int32, (8, heads * 128), 1)
    pick = jnp.where(c8 // 128 == r8, 1.0, 0.0).astype(BF)
    mean = (lax.dot_general(pick, hi, NT, preferred_element_type=F32)
            + lax.dot_general(pick, lo, NT, preferred_element_type=F32)) * (1.0 / 128)
    c = s_row * lax.rsqrt(s_row * s_row * mean + EPSILON) * (LOG2E / math.sqrt(128.0))
    r = lax.broadcasted_iota(jnp.int32, (8, rows), 0)
    both = jnp.where(r < heads, c, jnp.where(r == 6, s_row, 0.0))
    both = jnp.concatenate([both, jnp.zeros((8, 256 - rows), F32)], axis=1)
    hi8 = both.astype(BF).astype(F32)
    c16 = jnp.concatenate([hi8, both - hi8], axis=0)
    pay_ref[0:64, :] = pt[:, 0:128].astype(BF)
    lane = lax.broadcasted_iota(jnp.int32, (32, 128), 1)
    pay_ref[64:96, :] = jnp.where(lane < 64, pt[0:32, 128:256], pltpu.roll(pt[32:64, 128:256], 64, 1)).astype(BF)
    pay_ref[96:112, :] = c16[:, 0:128].astype(BF)
    pay_ref[112:128, :] = c16[:, 128:256].astype(BF)


def make_tokens(mine, other, w_in, embed, gain, akc, rows):
    vm = pl.BlockSpec(memory_space=pltpu.VMEM)
    width = w_in.shape[1]
    return pl.pallas_call(
        tokens_kernel,
        out_shape=(jax.ShapeDtypeStruct((rows, width), BF), jax.ShapeDtypeStruct((128, 128), BF)),
        in_specs=[vm] * 6,
        out_specs=(vm, vm),
        scratch_shapes=[pltpu.VMEM((rows, width), F32)],
        compiler_params=pltpu.CompilerParams(vmem_limit_bytes=24 << 20),
    )(mine, other, w_in, embed, gain, akc)


def query_kernel(tok_ref, wq_ref, qg_ref, kg_ref, akg_ref, qhat_ref, qop_ref, bound_ref):
    q = jnp.dot(tok_ref[...], wq_ref[...], preferred_element_type=F32)
    q = q * lax.rsqrt(jnp.mean(q * q, axis=1, keepdims=True) + EPSILON) * qg_ref[...]
    qb = q.astype(BF)
    qhat_ref[...] = qb
    qp = (lax.dot_general(qb, akg_ref[0], NT, preferred_element_type=F32)
          + lax.dot_general(qb, akg_ref[1], NT, preferred_element_type=F32))
    hi, lo = split(qp)
    qop_ref[:, 0:128] = hi
    qop_ref[:, 128:256] = lo
    reach = qb.astype(F32) * kg_ref[...]
    size = jnp.sqrt(jnp.sum(reach * reach, axis=1, keepdims=True)) * (LOG2E * 1.01)
    bound_ref[...] = jnp.broadcast_to(size, bound_ref.shape)


def make_query(tokens, w_query, q_gain, k_gain, akg):
    rows, width = tokens.shape
    heads = w_query.shape[1] // 128
    return pl.pallas_call(
        query_kernel,
        out_shape=(jax.ShapeDtypeStruct((rows, heads * 128), BF), jax.ShapeDtypeStruct((heads * rows, 256), BF),
                   jax.ShapeDtypeStruct((heads * rows, 128), F32)),
        grid=(heads,),
        in_specs=[
            pl.BlockSpec((rows, width), lambda h: (0, 0)),
            pl.BlockSpec((width, 128), lambda h: (0, h)),
            pl.BlockSpec((1, 128), lambda h: (0, 0)),
            pl.BlockSpec((1, 128), lambda h: (0, 0)),
            pl.BlockSpec((2, 128, 128), lambda h: (0, 0, h)),
        ],
        out_specs=(pl.BlockSpec((rows, 128), lambda h: (0, h)), pl.BlockSpec((rows, 256), lambda h: (h, 0)),
                   pl.BlockSpec((rows, 128), lambda h: (h, 0))),
        compiler_params=pltpu.CompilerParams(vmem_limit_bytes=24 << 20),
    )(tokens, w_query, q_gain, k_gain, akg)


def local(
    feats, conv_weight, conv_bias, latent_projection_weight, noise, step_index, hist, hist_level, hist_count,
    w_in, w_hist, norm_gain, w_query, w_key, w_value, q_gain, k_gain, w_out,
):
    grp = lax.axis_index("grp")
    seq_count = lax.axis_size("seq")
    frames, channels, pixels = feats.shape
    width = w_in.shape[1]
    head_size = q_gain.shape[0]
    heads = w_query.shape[1] // head_size
    half = w_out.shape[1] // 2
    rows = frames * pixels // 2

    earlier = lax.ppermute(feats, "seq", [(i, i + 1) for i in range(seq_count - 1)])

    spread = [jnp.where((hist_level == l)[:, None], hist, jnp.zeros_like(hist)) for l in range(3)]
    spread = jnp.concatenate([jnp.concatenate(spread[:2], axis=1), jnp.pad(spread[2], ((0, 0), (0, 64)))], axis=0)
    spread = gather_blocks(spread, seq_count, 1)
    slots = hist.shape[0]
    hx = jnp.concatenate([spread[:, :slots], spread[:, slots:, :64]], axis=2).reshape(seq_count * slots, 192)

    embed = time_embed(step_index, width)[None]
    gain = norm_gain[None]
    w_in = w_in.reshape(-1, 4, width).transpose(1, 0, 2).reshape(-1, width)
    kg = jnp.tile(k_gain, heads)[None]
    akc, akg, av, k_hist, v_hist = low_rank(w_in, gain, embed, hx, w_hist.reshape(-1, width), w_key, w_value, kg)

    sigma = (STEPS - step_index.astype(F32)) / STEPS
    mine = encode(earlier, feats, conv_weight, conv_bias[:, None], latent_projection_weight, noise, sigma)
    other = swap(mine)
    tokens, payload = make_tokens(mine, other, w_in, embed, gain, akc, rows)
    qhat, qop, bound = make_query(tokens, w_query, q_gain[None], k_gain[None], akg)
    gathered = gather_blocks(payload, seq_count, 0)

    live = jnp.arange(slots, dtype=jnp.int32)[None, :] < hist_count[:, None]
    hbias = jnp.broadcast_to(jnp.where(live, 0.0, -1e30).reshape(1, -1), (8, seq_count * slots)).astype(F32)

    w_far = swap(lax.dynamic_slice_in_dim(w_out, (1 - grp) * half, half, 1))
    w_near = lax.dynamic_slice_in_dim(w_out, grp * half, half, 1)

    heads_out = attend(gathered, qop, bound, qhat, k_hist, v_hist, hbias, av)
    heads_far = swap(heads_out)
    out = jnp.dot(heads_out, w_near, preferred_element_type=F32) + jnp.dot(heads_far, w_far, preferred_element_type=F32)
    return out.astype(BF)


def solution(mesh):
    placed = (
        P("seq", None, "grp"), P(), P(), P(), P("seq", None, "grp"), P(), P("seq", None), P("seq"), P(), P(), P(), P(),
        P(None, "grp"), P(None, "grp"), P(None, "grp"), P(), P(), P("grp", None),
    )
    return jax.shard_map(local, mesh=mesh, in_specs=placed, out_specs=P("seq", "grp"), check_vma=False)
```

```python
import functools
import math

import jax
import jax.numpy as jnp
from jax import lax
from jax.experimental import pallas as pl
from jax.experimental.pallas import tpu as pltpu
from jax.sharding import PartitionSpec as P

STEPS = 50
EPSILON = 1e-06
LOG2E = math.log2(math.e)
MESH = pl.DeviceIdType.MESH
BF = jnp.bfloat16
F32 = jnp.float32
LOW = -1e30


def split(x):
    hi = x.astype(BF)
    return hi, (x - hi.astype(F32)).astype(BF)


def unpack(block, kt_ref, vt_ref, c_ref):
    lane = lax.broadcasted_iota(jnp.int32, (64, 128), 1)
    lane16 = lax.broadcasted_iota(jnp.int32, (16, 128), 1)
    for pair in range(2):
        first, second = block[2 * pair].astype(F32), block[2 * pair + 1].astype(F32)

        def rest(x):
            low = x[64:96]
            return jnp.concatenate([low, pltpu.roll(low, 64, 1)], axis=0)

        tails = jnp.where(lane < 64, rest(first), pltpu.roll(rest(second), 64, 1))
        tail16 = jnp.where(lane16 < 64, first[112:128], pltpu.roll(second[112:128], 64, 1))
        parts = [
            (first[0:64], first[96:112]),
            (tails, tail16),
            (second[0:64], second[96:112]),
        ]
        for tile, (p, c16) in enumerate(parts):
            cols = slice((3 * pair + tile) * 128, (3 * pair + tile + 1) * 128)
            scales = c16[0:8] + c16[8:16]
            c_ref[:, cols] = scales
            pb = p.astype(BF)
            kt_ref[0:64, cols] = pb
            kt_ref[128:192, cols] = pb
            s_row = scales[6:7]
            vt_ref[0:64, cols] = (p * s_row).astype(BF)
            s_hi = c16[6:7]
            s_lo = c16[14:15]
            row = lax.broadcasted_iota(jnp.int32, (16, 128), 0)
            extra = jnp.where(row == 0, s_hi, jnp.where(row == 1, s_lo, jnp.where(row == 2, 1.0, 0.0)))
            vt_ref[64:80, cols] = extra.astype(BF)


NT = (((1,), (1,)), ((), ()))


def front_kernel(step_ref, level_ref, feats_ref, cw_ref, bias_ref, lw_ref, noise_ref, hist_ref, w_in_ref, wh_ref,
                 gain_ref, kg_ref, wk_hbm, wv_hbm, wout_hbm,
                 tok_ref, pay_ref, akg_ref, av_ref, akh_ref, avh_ref, far_ref,
                 early, wk, wv, acc_k, acc_v, x_ref, akc, w_perm, wave, mine, other,
                 wk_sem, wv_sem, send_sem, recv_sem):
    grp = lax.axis_index("grp")
    seq = lax.axis_index("seq")
    count = lax.axis_size("seq")
    core = seq % 2
    sibling = seq + 1 - 2 * core
    across = seq + 8 - 16 * ((seq // 8) % 2)
    after, before = (seq + 1) % count, (seq + count - 1) % count
    frames, channels, pixels = feats_ref.shape
    rows, width = tok_ref.shape
    cols = kg_ref.shape[1] * 6
    heads = cols // 128
    chunk = 512
    quarter = far_ref.shape[0] // 4
    half = far_ref.shape[1]

    loads = []
    for j in range(width // chunk):
        part = pl.ds(j * chunk, chunk)
        for source, into, sem in ((wk_hbm, wk, wk_sem), (wv_hbm, wv, wv_sem)):
            load = pltpu.make_async_copy(source.at[part], into.at[part], sem.at[j])
            load.start()
            loads.append(load)

    barrier = pltpu.get_barrier_semaphore()
    for there in ((1 - grp, seq), (1 - grp, across), (grp, sibling), (grp, after), (grp, before)):
        pl.semaphore_signal(barrier, inc=1, device_id=there, device_id_type=MESH)
    pl.semaphore_wait(barrier, 5)

    def send(n, source, into, there):
        return pltpu.make_async_remote_copy(
            src_ref=source, dst_ref=into, send_sem=send_sem.at[n], recv_sem=recv_sem.at[n],
            device_id=there, device_id_type=MESH)

    halo = send(0, feats_ref, early, (grp, after))
    halo.start()
    first_rows = pl.ds(pl.multiple_of(2 * core * quarter, quarter), quarter)
    second_rows = pl.ds(pl.multiple_of((2 * core + 1) * quarter, quarter), quarter)
    far_cols = pl.ds(pl.multiple_of((1 - grp) * half, half), half)
    piece_a = send(1, wout_hbm.at[first_rows, far_cols], far_ref.at[first_rows], (1 - grp, seq))
    piece_b = send(2, wout_hbm.at[second_rows, far_cols], far_ref.at[second_rows], (1 - grp, across))
    piece_a.start()
    piece_b.start()

    step = step_ref[0].astype(F32)
    place = lax.broadcasted_iota(jnp.int32, (8, width), 1)
    turn = jnp.where(place < width // 2, place, place - width // 2).astype(F32)
    angle = step * jnp.exp(turn * (-math.log(10000.0) / (width // 2)))
    wave[...] = jnp.where(place < width // 2, jnp.cos(angle), jnp.sin(angle))
    lane = lax.broadcasted_iota(jnp.int32, (16, 128), 1)
    line = lax.broadcasted_iota(jnp.int32, (16, 128), 0)
    level = jnp.zeros((16, 128), F32)
    for r in range(8):
        level = jnp.where(line == r, level_ref[r].astype(F32), level)
    base = jnp.concatenate([hist_ref[...].astype(F32), jnp.zeros((8, 64), F32)], axis=1)
    base = jnp.concatenate([base, jnp.zeros((8, 128), F32)], axis=0)
    moved = pltpu.roll(base, 64, 1)
    spread = jnp.concatenate([
        jnp.where(level == jnp.where(lane < 64, 0.0, 1.0), base + moved, 0.0),
        jnp.where(level == 2.0, base, 0.0)], axis=1).astype(BF)
    r64 = lax.broadcasted_iota(jnp.int32, (64, 64), 0)
    c64 = lax.broadcasted_iota(jnp.int32, (64, 64), 1)
    order = jnp.where(c64 == (r64 % 16) * 4 + r64 // 16, 1.0, 0.0).astype(BF)

    square = jnp.zeros((16, 1), F32)
    for j in range(width // chunk):
        part = slice(j * chunk, (j + 1) * chunk)
        gain = gain_ref[:, part]
        low = jnp.dot(order, w_in_ref[:, part], preferred_element_type=F32)
        w_perm[:, part] = low.astype(BF)
        low_hi, low_lo = split(low * gain)
        e_hi, e_lo = split(jnp.concatenate([wave[:, part]] * 2, axis=0) * gain)
        h = wh_ref[:, part]
        h_hi, h_lo = split(h.astype(F32) * gain)
        left = jnp.concatenate([low_hi, low_lo, e_hi, e_lo, h_hi, h_lo], axis=0)
        loads[2 * j].wait()
        k = jnp.dot(left, wk[part, :], preferred_element_type=F32)
        loads[2 * j + 1].wait()
        v = jnp.dot(left, wv[part, :], preferred_element_type=F32)
        acc_k[...] = k if j == 0 else acc_k[...] + k
        acc_v[...] = v if j == 0 else acc_v[...] + v
        raw = jnp.dot(spread[:, :192], h, preferred_element_type=F32)
        square = square + jnp.sum(raw * raw, axis=1, keepdims=True)

    def put(ref, full):
        hi, lo = split(full)
        ref[0] = hi
        ref[1] = lo

    def parts(acc):
        a = acc[0:64, :] + acc[64:128, :]
        b = acc[128:144, :] + acc[144:160, :]
        h = acc[160:352, :] + acc[352:544, :]
        h = jnp.concatenate([h, jnp.zeros((64, cols), F32)], axis=0)
        return a, b, lax.broadcasted_iota(jnp.int32, b.shape, 0), h

    kg = jnp.concatenate([kg_ref[...]] * heads, axis=1)
    pad = jnp.zeros((48, cols), F32)
    a, b, row, h = parts(acc_k)
    full = jnp.concatenate([a, jnp.where(row == 0, b, 0.0), pad], axis=0)
    put(akc, full)
    put(akg_ref, full * kg)
    put(akh_ref, h * kg)
    h_hi, h_lo = split(h)
    y = jnp.dot(spread, h_hi, preferred_element_type=F32) + jnp.dot(spread, h_lo, preferred_element_type=F32)
    s = lax.rsqrt(jnp.broadcast_to(square, (16, 128)) * (1.0 / width) + EPSILON)
    wide = jnp.where(lane == 70, s, 0.0)
    for head in range(heads):
        part = y[:, head * 128:(head + 1) * 128]
        mean = jnp.mean(part * part, axis=1, keepdims=True)
        wide = jnp.where(lane == 64 + head, s * lax.rsqrt(s * s * mean + EPSILON) * (LOG2E / math.sqrt(128.0)), wide)
    hi = wide.astype(BF).astype(F32)
    aux = jnp.where(lane == 80, level, hi + pltpu.roll(wide - hi, 8, 1))
    slots = jnp.concatenate([moved[0:8], aux[0:8]], axis=0)
    a, b, row, h = parts(acc_v)
    put(av_ref, jnp.concatenate([a, jnp.where(row < 2, b, 0.0), pad], axis=0))
    put(avh_ref, h)

    sigma = (STEPS - step) / STEPS
    bias = jnp.transpose(jnp.broadcast_to(bias_ref[...], (128, 128)))[:, 0:1]
    halo.wait_recv()
    lead = jnp.where(seq > 0, 1.0, 0.0)
    window = [jnp.where(lead > 0.5, early[0], jnp.zeros_like(early[0])),
              jnp.where(lead > 0.5, early[1], jnp.zeros_like(early[1])), feats_ref[0], feats_ref[1]]
    pixel = lax.broadcasted_iota(jnp.int32, (pixels, 256), 0)
    col = lax.broadcasted_iota(jnp.int32, (pixels, 256), 1)
    lines = [jnp.zeros((lw_ref.shape[0], 256), F32) for _ in range(4)]
    for t in range(frames):
        total = jnp.zeros((channels, pixels), F32)
        for tap in range(3):
            total = total + jnp.dot(cw_ref[tap], window[2 + t - tap], preferred_element_type=F32)
        total = total + bias
        hidden = (total * (1.0 / (1.0 + jnp.exp(-total)))).astype(BF)
        latent = jnp.dot(lw_ref[...], hidden, preferred_element_type=F32)
        noisy = ((1.0 - sigma) * latent + sigma * noise_ref[t].astype(F32)).astype(BF)
        for i in range(4):
            hit = (pixel % 4 == i) & (col == t * (pixels // 2) + grp * (pixels // 4) + pixel // 4)
            lines[i] = lines[i] + jnp.dot(noisy, jnp.where(hit, 1.0, 0.0).astype(BF), preferred_element_type=F32)
    mine[...] = jnp.concatenate(lines, axis=0).astype(BF)
    trade = send(3, mine, other, (1 - grp, seq))
    trade.start()
    piece_a.wait_recv()
    pass_a = send(4, far_ref.at[first_rows], far_ref.at[first_rows], (grp, sibling))
    pass_a.start()
    piece_b.wait_recv()
    pass_b = send(5, far_ref.at[second_rows], far_ref.at[second_rows], (grp, sibling))
    pass_b.start()
    trade.wait_recv()

    pt = mine[...].astype(F32) + other[...].astype(F32)
    row = lax.broadcasted_iota(jnp.int32, (64, 256), 0)
    tall = jnp.concatenate([pt, jnp.where(row == 0, 1.0, 0.0)], axis=0)
    px = jnp.transpose(tall)[:rows].astype(BF)
    p = px[:, :64]
    total = jnp.zeros((rows, 1), F32)
    total_row = jnp.zeros((8, rows), F32)
    ones = jnp.ones((8, chunk), BF)
    for j in range(width // chunk):
        part = slice(j * chunk, (j + 1) * chunk)
        x = jnp.dot(p, w_perm[:, part], preferred_element_type=F32) + wave[0:1, part]
        x_ref[:, part] = x
        x2 = x * x
        total = total + jnp.sum(x2, axis=1, keepdims=True)
        hi, lo = split(x2)
        total_row = total_row + lax.dot_general(ones, hi, NT, preferred_element_type=F32)
        total_row = total_row + lax.dot_general(ones, lo, NT, preferred_element_type=F32)
    s = lax.rsqrt(total * (1.0 / width) + EPSILON)
    s_row = lax.rsqrt(total_row * (1.0 / width) + EPSILON)
    y = jnp.dot(px, akc[0], preferred_element_type=F32) + jnp.dot(px, akc[1], preferred_element_type=F32)
    hi, lo = split(y * y)
    r8 = lax.broadcasted_iota(jnp.int32, (8, cols), 0)
    c8 = lax.broadcasted_iota(jnp.int32, (8, cols), 1)
    pick = jnp.where(c8 // 128 == r8, 1.0, 0.0).astype(BF)
    mean = (lax.dot_general(pick, hi, NT, preferred_element_type=F32)
            + lax.dot_general(pick, lo, NT, preferred_element_type=F32)) * (1.0 / 128)
    c = s_row * lax.rsqrt(s_row * s_row * mean + EPSILON) * (LOG2E / math.sqrt(128.0))
    r = lax.broadcasted_iota(jnp.int32, (8, rows), 0)
    both = jnp.where(r < heads, c, jnp.where(r == 6, s_row, 0.0))
    both = jnp.concatenate([both, jnp.zeros((8, 256 - rows), F32)], axis=1)
    hi8 = both.astype(BF).astype(F32)
    c16 = jnp.concatenate([hi8, both - hi8], axis=0)
    pay_ref[0:64, :] = pt[:, 0:128].astype(BF)
    lane32 = lax.broadcasted_iota(jnp.int32, (32, 128), 1)
    pay_ref[64:96, :] = jnp.where(lane32 < 64, pt[0:32, 128:256], pltpu.roll(pt[32:64, 128:256], 64, 1)).astype(BF)
    pay_ref[96:112, :] = c16[:, 0:128].astype(BF)
    pay_ref[112:128, :] = (c16[:, 128:256] + slots).astype(BF)
    for j in range(width // chunk):
        part = slice(j * chunk, (j + 1) * chunk)
        tok_ref[:, part] = (x_ref[:, part] * s * gain_ref[:, part]).astype(BF)

    pass_a.wait_recv()
    pass_b.wait_recv()
    for copy in (halo, piece_a, piece_b, trade, pass_a, pass_b):
        copy.wait_send()


def front(step_index, hist_level, feats, conv_weight, conv_bias, lat_weight, noise, hist, w_in, w_hist, gain, k_gain,
          w_key, w_value, w_out):
    rows = feats.shape[0] * feats.shape[2] // 2
    width, cols = w_key.shape
    vm = pl.BlockSpec(memory_space=pltpu.VMEM)
    sm = pl.BlockSpec(memory_space=pltpu.SMEM)
    hbm = pl.BlockSpec(memory_space=pl.ANY)
    dma = pltpu.SemaphoreType.DMA
    ops = jax.ShapeDtypeStruct((2, 128, cols), BF)
    big = jax.ShapeDtypeStruct((2, 256, cols), BF)
    return pl.pallas_call(
        front_kernel,
        out_shape=(jax.ShapeDtypeStruct((rows, width), BF), jax.ShapeDtypeStruct((128, 128), BF), ops, ops, big, big,
                   jax.ShapeDtypeStruct((w_out.shape[0], w_out.shape[1] // 2), BF)),
        in_specs=[sm, sm] + [vm] * 10 + [hbm] * 3,
        out_specs=(vm,) * 6 + (hbm,),
        scratch_shapes=[
            pltpu.VMEM(feats.shape, BF),
            pltpu.VMEM(w_key.shape, BF),
            pltpu.VMEM(w_value.shape, BF),
            pltpu.VMEM((544, cols), F32),
            pltpu.VMEM((544, cols), F32),
            pltpu.VMEM((rows, width), F32),
            pltpu.VMEM((2, 128, cols), BF),
            pltpu.VMEM((64, width), BF),
            pltpu.VMEM((8, width), F32),
            pltpu.VMEM((64, 256), BF),
            pltpu.VMEM((64, 256), BF),
            dma((6,)), dma((6,)), dma((6,)), dma((6,)),
        ],
        compiler_params=pltpu.CompilerParams(collective_id=1, has_side_effects=True, vmem_limit_bytes=60 << 20),
    )(step_index, hist_level, feats, conv_weight, conv_bias, lat_weight, noise, hist, w_in, w_hist, gain, k_gain,
      w_key, w_value, w_out)


def attend_kernel(chips, x_ref, tok_ref, wq_hbm, qg_ref, kg_ref, akg_ref, akh_ref, av_ref, avh_ref, live_ref, out_ref, theirs_ref,
                  g_ref, wq_ref, qop, qh, kt, vt, cs, acc, m_ref, hs, ax,
                  send_sem, recv_sem, fsend_sem, frecv_sem, osend_sem, orecv_sem, local_sem, wq_sem):
    grp = lax.axis_index("grp")
    seq = lax.axis_index("seq")
    core = seq % 2
    chip = seq // 2
    sibling = chip * 2 + 1 - core
    rows = tok_ref.shape[0]
    heads = wq_ref.shape[1] // 128
    group = kt.shape[1] // 384
    steps = chips // group

    def shift(k):
        z = (chip // 8 + k // 8) % 4
        x = (chip // 4 + k // 4) % 2
        y = (chip + k) % 4
        return (z * 2 + x) * 4 + y

    def back(k):
        z = (chip // 8 + 4 - k // 8) % 4
        x = (chip // 4 + k // 4) % 2
        y = (chip + 4 - k % 4) % 4
        return (z * 2 + x) * 4 + y

    load = pltpu.make_async_copy(wq_hbm, wq_ref, wq_sem)
    load.start()
    barrier = pltpu.get_barrier_semaphore()
    pl.semaphore_signal(barrier, inc=1, device_id=(grp, sibling), device_id_type=MESH)
    pl.semaphore_signal(barrier, inc=1, device_id=(1 - grp, seq), device_id_type=MESH)

    @pl.loop(1, chips)
    def _(k):
        pl.semaphore_signal(barrier, inc=1, device_id=(grp, shift(k) * 2 + core), device_id_type=MESH)

    pl.semaphore_wait(barrier, chips + 1)

    def direct(k):
        return pltpu.make_async_remote_copy(
            src_ref=x_ref, dst_ref=g_ref.at[seq], send_sem=send_sem.at[k], recv_sem=recv_sem.at[k],
            device_id=(grp, shift(k) * 2 + core), device_id_type=MESH)

    def forward(k):
        source = back(k) * 2 + core
        return pltpu.make_async_remote_copy(
            src_ref=g_ref.at[source], dst_ref=g_ref.at[source], send_sem=fsend_sem.at[k], recv_sem=frecv_sem.at[k],
            device_id=(grp, sibling), device_id_type=MESH)

    @pl.loop(1, chips)
    def _(k):
        direct(k).start()

    own = pltpu.make_async_copy(x_ref, g_ref.at[seq], local_sem)
    own.start()
    own.wait()
    forward(0).start()

    one_row = lax.broadcasted_iota(jnp.int32, (64, kt.shape[1]), 0)
    ones = jnp.where(one_row == 0, 1.0, 0.0).astype(BF)
    kt[64:128, :] = ones
    kt[192:256, :] = ones
    vt[80:128, :] = jnp.zeros((48, vt.shape[1]), BF)
    acc[...] = jnp.zeros_like(acc)
    m_ref[...] = jnp.full(m_ref.shape, LOW, F32)
    load.wait()
    for h in range(heads):
        sl = slice(h * rows, (h + 1) * rows)
        cols = slice(h * 128, (h + 1) * 128)
        q = jnp.dot(tok_ref[...], wq_ref[:, cols], preferred_element_type=F32)
        q = (q * lax.rsqrt(jnp.mean(q * q, axis=1, keepdims=True) + EPSILON) * qg_ref[...]).astype(BF)
        for ref, a_ref, n in ((qop, akg_ref, 128), (qh, akh_ref, 256)):
            qp = (lax.dot_general(q, a_ref[0, :, cols], NT, preferred_element_type=F32)
                  + lax.dot_general(q, a_ref[1, :, cols], NT, preferred_element_type=F32))
            hi, lo = split(qp)
            ref[sl, 0:n] = hi
            ref[sl, n:2 * n] = lo

    @pl.loop(1, group)
    def _(k):
        direct(k).wait_recv()
        forward(k).start()

    def absorb(h, s):
        sl = slice(h * rows, (h + 1) * rows)
        old = m_ref[sl, :]
        tiles = [s[:, j * 128:(j + 1) * 128] for j in range(s.shape[1] // 128)]
        top = functools.reduce(jnp.maximum, tiles)
        new = jnp.maximum(old, jnp.broadcast_to(jnp.max(top, axis=1, keepdims=True), old.shape))
        w = jnp.concatenate([jnp.exp2(t - new).astype(BF) for t in tiles], axis=1)
        m_ref[sl, :] = new
        return w, jnp.exp2(old - new)

    @pl.loop(0, steps)
    def _(i):
        for b in range(0, group, 2):
            places = []
            for k in (group * i + b, group * i + b + 1):
                forward(k).wait_recv()
                source = back(k) * 2
                places += [source, source + 1]
            cols = slice(b * 384, b * 384 + 768)
            unpack([g_ref[place] for place in places], kt.at[:, cols], vt.at[:, cols], cs.at[:, cols])

        def scores(h):
            return jnp.dot(qop[h * rows:(h + 1) * rows, :], kt[...], preferred_element_type=F32)

        def some(first, last):
            ahead = scores(first)
            for h in range(first, last):
                s = ahead
                if h + 1 < last:
                    ahead = scores(h + 1)
                sl = slice(h * rows, (h + 1) * rows)
                w, keep = absorb(h, s * cs[h:h + 1, :])
                acc[sl, :] = acc[sl, :] * keep + lax.dot_general(w, vt[...], NT, preferred_element_type=F32)

        some(0, heads // 2)

        @pl.when(i + 1 < steps)
        def _():
            for b in range(group):
                k = group * (i + 1) + b
                direct(k).wait_recv()
                forward(k).start()

        some(heads // 2, heads)

    @pl.loop(0, 2 * chips)
    def _(d):
        piece = pltpu.roll(g_ref[d, 112:128, :].astype(F32), 64, 1)
        spot = pl.ds(pl.multiple_of(d * 8, 8), 8)
        hs[spot, :] = piece[0:8]
        ax[spot, :] = piece[8:16]

    lane = lax.broadcasted_iota(jnp.int32, hs.shape, 1)
    level = ax[:, 16:17]
    size = ax[:, 6:7] + ax[:, 14:15]
    base = jnp.where(lane < 64, hs[...], 0.0)
    twice = base + pltpu.roll(base, 64, 1)
    first = jnp.where(level == jnp.where(lane < 64, 0.0, 1.0), twice, 0.0)
    second = jnp.where(level == 2.0, base, 0.0)
    kh = jnp.concatenate([first, second], axis=1).astype(BF)
    vh = jnp.concatenate([first * size, jnp.where(lane == 64, 1.0, second * size)], axis=1).astype(BF)
    across = jnp.transpose(ax[...])
    ch = across[0:8] + across[8:16]
    keys = kh.shape[0]
    owner = lax.broadcasted_iota(jnp.int32, (keys // 8, keys), 0)
    slot = lax.broadcasted_iota(jnp.int32, (keys // 8, keys), 1)
    counts = jnp.dot(jnp.broadcast_to(live_ref[...], (8, keys // 8)).astype(F32).astype(BF),
                     jnp.where(slot // 8 == owner, 1.0, 0.0).astype(BF), preferred_element_type=F32)
    hbias = jnp.where((slot[0:1] % 8).astype(F32) < counts[0:1], 0.0, LOW)

    def share(h):
        cols = slice(h * 128, (h + 1) * 128)
        return pltpu.make_async_remote_copy(
            src_ref=out_ref.at[:, cols], dst_ref=theirs_ref.at[:, cols], send_sem=osend_sem.at[h],
            recv_sem=orecv_sem.at[h], device_id=(1 - grp, seq), device_id_type=MESH)

    for h in range(heads):
        sl = slice(h * rows, (h + 1) * rows)
        cols = slice(h * 128, (h + 1) * 128)
        s = (lax.dot_general(qh[sl, 0:256], kh, NT, preferred_element_type=F32)
             + lax.dot_general(qh[sl, 256:512], kh, NT, preferred_element_type=F32))
        w, keep = absorb(h, s * ch[h:h + 1, :] + hbias)
        a = acc[sl, :] * keep
        b = jnp.dot(w, vh, preferred_element_type=F32)
        o = jnp.zeros((rows, 128), F32)
        for part, ref in ((a, av_ref), (b, avh_ref)):
            hi, lo = split(part)
            o = o + jnp.dot(hi, ref[0, :, cols], preferred_element_type=F32)
            o = o + jnp.dot(lo, ref[0, :, cols], preferred_element_type=F32)
            o = o + jnp.dot(hi, ref[1, :, cols], preferred_element_type=F32)
        out_ref[:, cols] = (o / (a[:, 66:67] + b[:, 192:193])).astype(BF)
        share(h).start()

    @pl.loop(0, chips)
    def _(k):
        forward(k).wait_send()

    @pl.loop(1, chips)
    def _(k):
        direct(k).wait_send()

    for h in range(heads):
        share(h).wait()


def attend(payload, tokens, w_query, q_gain, k_gain, akg, akh, av, avh, live, count):
    chips = count // 2
    rows = tokens.shape[0]
    cols = w_query.shape[1]
    tall = rows * cols // 128
    vm = pl.BlockSpec(memory_space=pltpu.VMEM)
    dma = pltpu.SemaphoreType.DMA
    return pl.pallas_call(
        functools.partial(attend_kernel, chips),
        out_shape=(jax.ShapeDtypeStruct((rows, cols), BF),) * 2,
        in_specs=[vm, vm, pl.BlockSpec(memory_space=pl.ANY)] + [vm] * 7,
        out_specs=(vm, vm),
        scratch_shapes=[
            pltpu.VMEM((count,) + payload.shape, BF),
            pltpu.VMEM(w_query.shape, BF),
            pltpu.VMEM((tall, 256), BF),
            pltpu.VMEM((tall, 512), BF),
            pltpu.VMEM((256, 1536), BF),
            pltpu.VMEM((128, 1536), BF),
            pltpu.VMEM((8, 1536), F32),
            pltpu.VMEM((tall, 128), F32),
            pltpu.VMEM((tall, 128), F32),
            pltpu.VMEM((count * 8, 128), F32),
            pltpu.VMEM((count * 8, 128), F32),
            dma((chips,)), dma((chips,)), dma((chips,)), dma((chips,)), dma((cols // 128,)), dma((cols // 128,)), dma, dma,
        ],
        compiler_params=pltpu.CompilerParams(collective_id=0, has_side_effects=True, vmem_limit_bytes=60 << 20),
    )(payload, tokens, w_query, q_gain, k_gain, akg, akh, av, avh, live)


def out_kernel(grp_ref, near_ref, theirs_ref, w_ref, far_ref, out_ref):
    out = jnp.dot(near_ref[...], w_ref[...], preferred_element_type=F32)
    out = out + jnp.dot(theirs_ref[...], far_ref[...], preferred_element_type=F32)
    out_ref[...] = out.astype(BF)


def project(near, theirs, w_out, far):
    rows, deep = near.shape
    half = far.shape[1]
    block = 256
    whole = pl.BlockSpec((rows, deep), lambda j, g: (0, 0))
    return pl.pallas_call(
        out_kernel,
        out_shape=jax.ShapeDtypeStruct((rows, half), BF),
        grid_spec=pltpu.PrefetchScalarGridSpec(
            num_scalar_prefetch=1,
            grid=(half // block,),
            in_specs=[
                whole, whole,
                pl.BlockSpec((deep, block), lambda j, g: (0, g[0] * (half // block) + j)),
                pl.BlockSpec((deep, block), lambda j, g: (0, j)),
            ],
            out_specs=pl.BlockSpec((rows, block), lambda j, g: (0, j)),
        ),
        compiler_params=pltpu.CompilerParams(vmem_limit_bytes=60 << 20),
    )(lax.axis_index("grp").astype(jnp.int32)[None], near, theirs, w_out, far)


def local(
    feats, conv_weight, conv_bias, latent_projection_weight, noise, step_index, hist, hist_level, hist_count,
    w_in, w_hist, norm_gain, w_query, w_key, w_value, q_gain, k_gain, w_out,
):
    width = w_in.shape[1]
    tokens, payload, akg, av, akh, avh, far = front(
        step_index, hist_level, feats, conv_weight, conv_bias[None], latent_projection_weight, noise, hist, w_in,
        w_hist.reshape(-1, width), norm_gain[None], k_gain[None], w_key, w_value, w_out)
    near, theirs = attend(
        payload, tokens, w_query, q_gain[None], k_gain[None], akg, akh, av, avh, hist_count[None], lax.axis_size("seq"))
    return project(near, theirs, w_out, far)


def solution(mesh):
    placed = (
        P("seq", None, "grp"), P(), P(), P(), P("seq", None, "grp"), P(), P("seq", None), P("seq"), P(), P(), P(), P(),
        P(None, "grp"), P(None, "grp"), P(None, "grp"), P(), P(), P("grp", None),
    )
    return jax.shard_map(local, mesh=mesh, in_specs=placed, out_specs=P("seq", "grp"), check_vma=False)
```

```python
import functools
import math

import jax
import jax.numpy as jnp
from jax import lax
from jax.experimental import pallas as pl
from jax.experimental.pallas import tpu as pltpu
from jax.sharding import PartitionSpec as P

STEPS = 50
EPSILON = 1e-06
LOG2E = math.log2(math.e)
MESH = pl.DeviceIdType.MESH
BF = jnp.bfloat16
F32 = jnp.float32
LOW = -1e30


def split(x):
    hi = x.astype(BF)
    return hi, (x - hi.astype(F32)).astype(BF)


def unpack(block, kt_ref, vt_ref, c_ref):
    lane = lax.broadcasted_iota(jnp.int32, (64, 128), 1)
    lane16 = lax.broadcasted_iota(jnp.int32, (16, 128), 1)
    for pair in range(2):
        first, second = block[2 * pair].astype(F32), block[2 * pair + 1].astype(F32)

        def rest(x):
            low = x[64:96]
            return jnp.concatenate([low, pltpu.roll(low, 64, 1)], axis=0)

        tails = jnp.where(lane < 64, rest(first), pltpu.roll(rest(second), 64, 1))
        tail16 = jnp.where(lane16 < 64, first[112:128], pltpu.roll(second[112:128], 64, 1))
        parts = [
            (first[0:64], first[96:112]),
            (tails, tail16),
            (second[0:64], second[96:112]),
        ]
        for tile, (p, c16) in enumerate(parts):
            cols = slice((3 * pair + tile) * 128, (3 * pair + tile + 1) * 128)
            scales = c16[0:8] + c16[8:16]
            c_ref[:, cols] = scales
            pb = p.astype(BF)
            kt_ref[0:64, cols] = pb
            kt_ref[128:192, cols] = pb
            s_row = scales[6:7]
            vt_ref[0:64, cols] = (p * s_row).astype(BF)
            s_hi = c16[6:7]
            s_lo = c16[14:15]
            row = lax.broadcasted_iota(jnp.int32, (16, 128), 0)
            extra = jnp.where(row == 0, s_hi, jnp.where(row == 1, s_lo, jnp.where(row == 2, 1.0, 0.0)))
            vt_ref[64:80, cols] = extra.astype(BF)


NT = (((1,), (1,)), ((), ()))


def section_kernel(step_ref, level_ref, feats_ref, cw_ref, bias_ref, lw_ref, noise_ref, hist_ref, w_in_ref, wh_ref,
                   gain_ref, kg_ref, qg_ref, live_ref, wq_hbm, wk_hbm, wv_hbm, wout_hbm, out_ref,
                   early, wk, wv, acc_k, acc_v, x_ref, akc, w_perm, wave, mine, other, far_ref, near_ref,
                   tok_ref, pay_ref, lefts, akg_ref, av_ref, akh_ref, avh_ref,
                   g_ref, wq_ref, qop, qh, kt, vt, cs, acc, m_ref, hs, ax, own, theirs,
                   wk_sem, wv_sem, tsend_sem, trecv_sem, load_sem,
                   send_sem, recv_sem, fsend_sem, frecv_sem, osend_sem, orecv_sem):
    grp = lax.axis_index("grp")
    seq = lax.axis_index("seq")
    count = lax.axis_size("seq")
    core = seq % 2
    sibling = seq + 1 - 2 * core
    across = seq + 8 - 16 * ((seq // 8) % 2)
    after, before = (seq + 1) % count, (seq + count - 1) % count
    chip = seq // 2
    chips = count // 2
    frames, pixels, channels = feats_ref.shape
    rows, width = tok_ref.shape
    group = kt.shape[1] // 384
    steps = chips // group

    def shift(k):
        z = (chip // 8 + (k // 4) % 4) % 4
        x = (chip // 4 + k // 16) % 2
        y = (chip + k) % 4
        return (z * 2 + x) * 4 + y

    def back(k):
        z = (chip // 8 + 4 - (k // 4) % 4) % 4
        x = (chip // 4 + k // 16) % 2
        y = (chip + 4 - k % 4) % 4
        return (z * 2 + x) * 4 + y

    cols = kg_ref.shape[1] * 6
    heads = cols // 128
    chunk = 512
    quarter = far_ref.shape[0] // 4
    half = far_ref.shape[1]

    def chunk_load(source, into, sem, j):
        part = pl.ds(j * chunk, chunk)
        return pltpu.make_async_copy(source.at[part], into.at[part], sem.at[j])

    key_loads = [chunk_load(wk_hbm, wk, wk_sem, j) for j in range(width // chunk)]
    value_loads = [chunk_load(wv_hbm, wv, wv_sem, j) for j in range(width // chunk)]
    for load in key_loads + value_loads:
        load.start()

    barrier = pltpu.get_barrier_semaphore()
    for there in ((1 - grp, seq), (1 - grp, across), (grp, sibling), (grp, after), (grp, before)):
        pl.semaphore_signal(barrier, inc=1, device_id=there, device_id_type=MESH)

    plane = chips // 2

    @pl.loop(1, plane + 1)
    def _(k):
        pl.semaphore_signal(barrier, inc=1, device_id=(grp, shift(k) * 2 + core), device_id_type=MESH)

    pl.semaphore_wait(barrier, plane + 5)

    def send(n, source, into, there):
        return pltpu.make_async_remote_copy(
            src_ref=source, dst_ref=into, send_sem=tsend_sem.at[n], recv_sem=trecv_sem.at[n],
            device_id=there, device_id_type=MESH)

    halo = send(0, feats_ref, early, (grp, after))
    halo.start()
    first_rows = pl.ds(pl.multiple_of(2 * core * quarter, quarter), quarter)
    second_rows = pl.ds(pl.multiple_of((2 * core + 1) * quarter, quarter), quarter)
    far_cols = pl.ds(pl.multiple_of((1 - grp) * half, half), half)
    piece_a = send(1, wout_hbm.at[first_rows, far_cols], far_ref.at[first_rows], (1 - grp, seq))
    piece_b = send(2, wout_hbm.at[second_rows, far_cols], far_ref.at[second_rows], (1 - grp, across))

    step = step_ref[0].astype(F32)
    place = lax.broadcasted_iota(jnp.int32, (8, width), 1)
    turn = jnp.where(place < width // 2, place, place - width // 2).astype(F32)
    angle = step * jnp.exp(turn * (-math.log(10000.0) / (width // 2)))
    wave[...] = jnp.where(place < width // 2, jnp.cos(angle), jnp.sin(angle))
    lane = lax.broadcasted_iota(jnp.int32, (16, 128), 1)
    line = lax.broadcasted_iota(jnp.int32, (16, 128), 0)
    level = jnp.zeros((16, 128), F32)
    for r in range(8):
        level = jnp.where(line == r, level_ref[r].astype(F32), level)
    base = jnp.concatenate([hist_ref[...].astype(F32), jnp.zeros((8, 64), F32)], axis=1)
    base = jnp.concatenate([base, jnp.zeros((8, 128), F32)], axis=0)
    moved = pltpu.roll(base, 64, 1)
    spread = jnp.concatenate([
        jnp.where(level == jnp.where(lane < 64, 0.0, 1.0), base + moved, 0.0),
        jnp.where(level == 2.0, base, 0.0)], axis=1).astype(BF)
    r64 = lax.broadcasted_iota(jnp.int32, (64, 64), 0)
    c64 = lax.broadcasted_iota(jnp.int32, (64, 64), 1)
    order = jnp.where(c64 == (r64 % 16) * 4 + r64 // 16, 1.0, 0.0).astype(BF)

    square = jnp.zeros((16, 1), F32)
    for j in range(width // chunk):
        part = slice(j * chunk, (j + 1) * chunk)
        gain = gain_ref[:, part]
        low = jnp.dot(order, w_in_ref[:, part], preferred_element_type=F32)
        w_perm[:, part] = low.astype(BF)
        low_hi, low_lo = split(low * gain)
        e_hi, e_lo = split(jnp.concatenate([wave[:, part]] * 2, axis=0) * gain)
        raw = jnp.dot(spread[:, :192], wh_ref[:, part], preferred_element_type=F32)
        square = square + jnp.sum(raw * raw, axis=1, keepdims=True)
        r_hi, r_lo = split(raw * gain)
        base_rows = jnp.concatenate([low_hi, low_lo, e_hi, e_lo], axis=0)
        lefts[:, part] = base_rows
        key_loads[j].wait()
        k = jnp.dot(jnp.concatenate([base_rows, r_hi, r_lo], axis=0), wk[part, :], preferred_element_type=F32)
        acc_k[0:192, :] = k if j == 0 else acc_k[0:192, :] + k

    def put(ref, full):
        hi, lo = split(full)
        ref[0] = hi
        ref[1] = lo

    def low_parts(acc):
        a = acc[0:64, :] + acc[64:128, :]
        b = acc[128:144, :] + acc[144:160, :]
        return a, b, lax.broadcasted_iota(jnp.int32, b.shape, 0)

    kg = jnp.concatenate([kg_ref[...]] * heads, axis=1)
    pad = jnp.zeros((48, cols), F32)
    a, b, row = low_parts(acc_k)
    full = jnp.concatenate([a, jnp.where(row == 0, b, 0.0), pad], axis=0)
    put(akc, full)
    put(akg_ref, full * kg)
    y = acc_k[160:176, :] + acc_k[176:192, :]
    s = lax.rsqrt(jnp.broadcast_to(square, (16, 128)) * (1.0 / width) + EPSILON)
    wide = jnp.where(lane == 70, s, 0.0)
    for head in range(heads):
        part = y[:, head * 128:(head + 1) * 128]
        mean = jnp.mean(part * part, axis=1, keepdims=True)
        wide = jnp.where(lane == 64 + head, s * lax.rsqrt(s * s * mean + EPSILON) * (LOG2E / math.sqrt(128.0)), wide)
    hi = wide.astype(BF).astype(F32)
    aux = jnp.where(lane == 80, level, hi + pltpu.roll(wide - hi, 8, 1))
    slots = jnp.concatenate([moved[0:8], aux[0:8]], axis=0)

    load_query = pltpu.make_async_copy(wq_hbm, wq_ref, load_sem.at[0])
    load_query.start()
    near_cols = pl.ds(pl.multiple_of(grp * half, half), half)
    load_near = pltpu.make_async_copy(wout_hbm.at[:, near_cols], near_ref, load_sem.at[1])
    load_near.start()
    sigma = (STEPS - step) / STEPS
    bias = jnp.transpose(jnp.broadcast_to(bias_ref[...], (128, 128)))[:, 0:1]
    halo.wait_recv()
    lead = jnp.where(seq > 0, 1.0, 0.0)
    window = [jnp.where(lead > 0.5, early[0], jnp.zeros_like(early[0])),
              jnp.where(lead > 0.5, early[1], jnp.zeros_like(early[1])), feats_ref[0], feats_ref[1]]
    pixel = lax.broadcasted_iota(jnp.int32, (pixels, 256), 0)
    col = lax.broadcasted_iota(jnp.int32, (pixels, 256), 1)
    lines = [jnp.zeros((lw_ref.shape[0], 256), F32) for _ in range(4)]
    for t in range(frames):
        total = jnp.zeros((channels, pixels), F32)
        for tap in range(3):
            total = total + lax.dot_general(cw_ref[tap], window[2 + t - tap], NT, preferred_element_type=F32)
        total = total + bias
        hidden = (total * (1.0 / (1.0 + jnp.exp(-total)))).astype(BF)
        latent = jnp.dot(lw_ref[...], hidden, preferred_element_type=F32)
        noisy = ((1.0 - sigma) * latent + sigma * noise_ref[t].astype(F32)).astype(BF)
        for i in range(4):
            hit = (pixel % 4 == i) & (col == t * (pixels // 2) + grp * (pixels // 4) + pixel // 4)
            lines[i] = lines[i] + jnp.dot(noisy, jnp.where(hit, 1.0, 0.0).astype(BF), preferred_element_type=F32)
    mine[...] = jnp.concatenate(lines, axis=0).astype(BF)
    trade = send(3, mine, other, (1 - grp, seq))
    trade.start()
    pass_a = send(4, far_ref.at[first_rows], far_ref.at[first_rows], (grp, sibling))
    pass_b = send(5, far_ref.at[second_rows], far_ref.at[second_rows], (grp, sibling))
    trade.wait_recv()

    pt = mine[...].astype(F32) + other[...].astype(F32)
    row = lax.broadcasted_iota(jnp.int32, (64, 256), 0)
    tall = jnp.concatenate([pt, jnp.where(row == 0, 1.0, 0.0)], axis=0)
    px = jnp.transpose(tall)[:rows].astype(BF)
    p = px[:, :64]
    total = jnp.zeros((rows, 1), F32)
    total_row = jnp.zeros((8, rows), F32)
    ones = jnp.ones((8, chunk), BF)
    for j in range(width // chunk):
        part = slice(j * chunk, (j + 1) * chunk)
        x = jnp.dot(p, w_perm[:, part], preferred_element_type=F32) + wave[0:1, part]
        x_ref[:, part] = x
        x2 = x * x
        total = total + jnp.sum(x2, axis=1, keepdims=True)
        hi, lo = split(x2)
        total_row = total_row + lax.dot_general(ones, hi, NT, preferred_element_type=F32)
        total_row = total_row + lax.dot_general(ones, lo, NT, preferred_element_type=F32)
    s = lax.rsqrt(total * (1.0 / width) + EPSILON)
    s_row = lax.rsqrt(total_row * (1.0 / width) + EPSILON)
    y = jnp.dot(px, akc[0], preferred_element_type=F32) + jnp.dot(px, akc[1], preferred_element_type=F32)
    hi, lo = split(y * y)
    r8 = lax.broadcasted_iota(jnp.int32, (8, cols), 0)
    c8 = lax.broadcasted_iota(jnp.int32, (8, cols), 1)
    pick = jnp.where(c8 // 128 == r8, 1.0, 0.0).astype(BF)
    mean = (lax.dot_general(pick, hi, NT, preferred_element_type=F32)
            + lax.dot_general(pick, lo, NT, preferred_element_type=F32)) * (1.0 / 128)
    c = s_row * lax.rsqrt(s_row * s_row * mean + EPSILON) * (LOG2E / math.sqrt(128.0))
    r = lax.broadcasted_iota(jnp.int32, (8, rows), 0)
    both = jnp.where(r < heads, c, jnp.where(r == 6, s_row, 0.0))
    both = jnp.concatenate([both, jnp.zeros((8, 256 - rows), F32)], axis=1)
    hi8 = both.astype(BF).astype(F32)
    c16 = jnp.concatenate([hi8, both - hi8], axis=0)
    pay_ref[0:64, :] = pt[:, 0:128].astype(BF)
    lane32 = lax.broadcasted_iota(jnp.int32, (32, 128), 1)
    pay_ref[64:96, :] = jnp.where(lane32 < 64, pt[0:32, 128:256], pltpu.roll(pt[32:64, 128:256], 64, 1)).astype(BF)
    pay_ref[96:112, :] = c16[:, 0:128].astype(BF)
    pay_ref[112:128, :] = (c16[:, 128:256] + slots).astype(BF)
    def direct(k):
        return pltpu.make_async_remote_copy(
            src_ref=pay_ref, dst_ref=g_ref.at[seq], send_sem=send_sem.at[k], recv_sem=recv_sem.at[k],
            device_id=(grp, shift(k) * 2 + core), device_id_type=MESH)

    def forward(k):
        source = back(k) * 2 + core
        return pltpu.make_async_remote_copy(
            src_ref=g_ref.at[source], dst_ref=g_ref.at[source], send_sem=fsend_sem.at[k], recv_sem=frecv_sem.at[k],
            device_id=(grp, sibling), device_id_type=MESH)

    facing = back(plane) * 2 + core

    def relay(k):
        return pltpu.make_async_remote_copy(
            src_ref=g_ref.at[facing], dst_ref=g_ref.at[facing], send_sem=send_sem.at[k], recv_sem=recv_sem.at[k],
            device_id=(grp, shift(k - plane) * 2 + core), device_id_type=MESH)

    direct(plane).start()

    @pl.loop(1, plane)
    def _(k):
        direct(k).start()

    here = pltpu.make_async_copy(pay_ref, g_ref.at[seq], load_sem.at[2])
    here.start()
    here.wait()
    forward(0).start()

    for j in range(width // chunk):
        part = slice(j * chunk, (j + 1) * chunk)
        tok_ref[:, part] = (x_ref[:, part] * s * gain_ref[:, part]).astype(BF)

    one_row = lax.broadcasted_iota(jnp.int32, (64, kt.shape[1]), 0)
    ones = jnp.where(one_row == 0, 1.0, 0.0).astype(BF)
    kt[64:128, :] = ones
    kt[192:256, :] = ones
    vt[80:128, :] = jnp.zeros((48, vt.shape[1]), BF)
    acc[...] = jnp.zeros_like(acc)
    m_ref[...] = jnp.full(m_ref.shape, LOW, F32)
    direct(plane).wait_recv()
    forward(plane).start()

    @pl.loop(plane + 1, chips)
    def _(k):
        relay(k).start()

    for j in range(width // chunk):
        part = slice(j * chunk, (j + 1) * chunk)
        h_hi, h_lo = split(wh_ref[:, part].astype(F32) * gain_ref[:, part])
        both_h = jnp.concatenate([h_hi, h_lo], axis=0)
        k = jnp.dot(both_h, wk[part, :], preferred_element_type=F32)
        value_loads[j].wait()
        v = jnp.dot(jnp.concatenate([lefts[:, part], both_h], axis=0), wv[part, :], preferred_element_type=F32)
        acc_k[0:384, :] = k if j == 0 else acc_k[0:384, :] + k
        acc_v[...] = v if j == 0 else acc_v[...] + v
    pad_h = jnp.zeros((64, cols), F32)
    put(akh_ref, jnp.concatenate([acc_k[0:192, :] + acc_k[192:384, :], pad_h], axis=0) * kg)
    a, b, row = low_parts(acc_v)
    put(av_ref, jnp.concatenate([a, jnp.where(row < 2, b, 0.0), pad], axis=0))
    put(avh_ref, jnp.concatenate([acc_v[160:352, :] + acc_v[352:544, :], pad_h], axis=0))

    @pl.loop(1, group)
    def _(k):
        direct(k).wait_recv()
        forward(k).start()

    load_query.wait()
    for h in range(heads):
        sl = slice(h * rows, (h + 1) * rows)
        cols = slice(h * 128, (h + 1) * 128)
        q = jnp.dot(tok_ref[...], wq_ref[:, cols], preferred_element_type=F32)
        q = (q * lax.rsqrt(jnp.mean(q * q, axis=1, keepdims=True) + EPSILON) * qg_ref[...]).astype(BF)
        for ref, a_ref, n in ((qop, akg_ref, 128), (qh, akh_ref, 256)):
            qp = (lax.dot_general(q, a_ref[0, :, cols], NT, preferred_element_type=F32)
                  + lax.dot_general(q, a_ref[1, :, cols], NT, preferred_element_type=F32))
            hi, lo = split(qp)
            ref[sl, 0:n] = hi
            ref[sl, n:2 * n] = lo

    @pl.loop(group, 2 * group)
    def _(k):
        direct(k).wait_recv()
        forward(k).start()

    def absorb(h, s):
        sl = slice(h * rows, (h + 1) * rows)
        old = m_ref[sl, :]
        tiles = [s[:, j * 128:(j + 1) * 128] for j in range(s.shape[1] // 128)]
        top = functools.reduce(jnp.maximum, tiles)
        new = jnp.maximum(old, jnp.broadcast_to(jnp.max(top, axis=1, keepdims=True), old.shape))
        w = jnp.concatenate([jnp.exp2(t - new).astype(BF) for t in tiles], axis=1)
        m_ref[sl, :] = new
        return w, jnp.exp2(old - new)

    def take(i):
        for b in range(0, group, 2):
            places = []
            for k in (group * i + b, group * i + b + 1):
                forward(k).wait_recv()
                source = back(k) * 2
                places += [source, source + 1]
            lot = slice(b * 384, b * 384 + 768)
            unpack([g_ref[place] for place in places], kt.at[:, lot], vt.at[:, lot], cs.at[:, lot])

    def scores(h):
        return jnp.dot(qop[h * rows:(h + 1) * rows, :], kt[...], preferred_element_type=F32)

    @pl.loop(0, steps - 1)
    def _(i):
        take(i)

        def some(first, last):
            ahead = scores(first)
            for h in range(first, last):
                s = ahead
                if h + 1 < last:
                    ahead = scores(h + 1)
                sl = slice(h * rows, (h + 1) * rows)
                w, keep = absorb(h, s * cs[h:h + 1, :])
                acc[sl, :] = acc[sl, :] * keep + lax.dot_general(w, vt[...], NT, preferred_element_type=F32)

        some(0, heads // 2)

        @pl.when((i + 2 < steps) & (i + 2 != steps // 2))
        def _():
            for b in range(group):
                k = group * (i + 2) + b
                direct(k).wait_recv()
                forward(k).start()

        @pl.when(i + 2 == steps // 2)
        def _():
            for b in range(1, group):
                k = plane + b
                direct(k).wait_recv()
                forward(k).start()

        @pl.when(i == 0)
        def _():
            piece_a.start()
            piece_b.start()

        @pl.when(i == steps - 2)
        def _():
            piece_a.wait_recv()
            pass_a.start()
            piece_b.wait_recv()
            pass_b.start()

        some(heads // 2, heads)

    take(steps - 1)

    @pl.loop(0, chips // 4)
    def _(n):
        for b in range(8):
            piece = pltpu.roll(g_ref[n * 8 + b, 112:128, :].astype(F32), 64, 1)
            spot = pl.ds(pl.multiple_of(n * 64 + b * 8, 8), 8)
            hs[spot, :] = piece[0:8]
            ax[spot, :] = piece[8:16]

    lane = lax.broadcasted_iota(jnp.int32, hs.shape, 1)
    level = ax[:, 16:17]
    size = ax[:, 6:7] + ax[:, 14:15]
    base = jnp.where(lane < 64, hs[...], 0.0)
    twice = base + pltpu.roll(base, 64, 1)
    first = jnp.where(level == jnp.where(lane < 64, 0.0, 1.0), twice, 0.0)
    second = jnp.where(level == 2.0, base, 0.0)
    kh = jnp.concatenate([first, second], axis=1).astype(BF)
    vh = jnp.concatenate([first * size, jnp.where(lane == 64, 1.0, second * size)], axis=1).astype(BF)
    across = jnp.transpose(ax[...])
    ch = across[0:8] + across[8:16]
    keys = kh.shape[0]
    owner = lax.broadcasted_iota(jnp.int32, (keys // 8, keys), 0)
    slot = lax.broadcasted_iota(jnp.int32, (keys // 8, keys), 1)
    counts = jnp.dot(jnp.broadcast_to(live_ref[...], (8, keys // 8)).astype(F32).astype(BF),
                     jnp.where(slot // 8 == owner, 1.0, 0.0).astype(BF), preferred_element_type=F32)
    hbias = jnp.where((slot[0:1] % 8).astype(F32) < counts[0:1], 0.0, LOW)

    def hist_scores(h):
        sl = slice(h * rows, (h + 1) * rows)
        return (lax.dot_general(qh[sl, 0:256], kh, NT, preferred_element_type=F32)
                + lax.dot_general(qh[sl, 256:512], kh, NT, preferred_element_type=F32))

    def share(h):
        lot = slice(h * 128, (h + 1) * 128)
        return pltpu.make_async_remote_copy(
            src_ref=own.at[:, lot], dst_ref=theirs.at[:, lot], send_sem=osend_sem.at[h],
            recv_sem=orecv_sem.at[h], device_id=(1 - grp, seq), device_id_type=MESH)

    def both_scores(h):
        return scores(h), hist_scores(h)

    ahead = both_scores(0)
    for h in range(heads):
        s, t = ahead
        if h + 1 < heads:
            ahead = both_scores(h + 1)
        sl = slice(h * rows, (h + 1) * rows)
        lot = slice(h * 128, (h + 1) * 128)
        wide_s = jnp.concatenate([s * cs[h:h + 1, :], t * ch[h:h + 1, :] + hbias], axis=1)
        w, keep = absorb(h, wide_s)
        n = s.shape[1]
        a = acc[sl, :] * keep + lax.dot_general(w[:, :n], vt[...], NT, preferred_element_type=F32)
        b = jnp.dot(w[:, n:], vh, preferred_element_type=F32)
        if h > 0:
            share(h - 1).start()
        o = jnp.zeros((rows, 128), F32)
        for value, weight in ((a, av_ref), (b, avh_ref)):
            hi, lo = split(value)
            o = o + jnp.dot(hi, weight[0, :, lot], preferred_element_type=F32)
            o = o + jnp.dot(lo, weight[0, :, lot], preferred_element_type=F32)
            o = o + jnp.dot(hi, weight[1, :, lot], preferred_element_type=F32)
        own[:, lot] = (o / (a[:, 66:67] + b[:, 192:193])).astype(BF)
    share(heads - 1).start()

    load_near.wait()
    for j in range(half // chunk):
        part = slice(j * chunk, (j + 1) * chunk)
        x_ref[:, part] = jnp.dot(own[...], near_ref[:, part], preferred_element_type=F32)
    pass_a.wait_recv()
    pass_b.wait_recv()
    for h in range(heads):
        share(h).wait_recv()
    for j in range(half // chunk):
        part = slice(j * chunk, (j + 1) * chunk)
        out_ref[:, part] = (x_ref[:, part]
                            + jnp.dot(theirs[...], far_ref[:, part], preferred_element_type=F32)).astype(BF)

    @pl.loop(0, chips)
    def _(k):
        forward(k).wait_send()

    @pl.loop(1, plane + 1)
    def _(k):
        direct(k).wait_send()

    @pl.loop(plane + 1, chips)
    def _(k):
        relay(k).wait_send()

    for h in range(heads):
        share(h).wait_send()
    for copy in (halo, piece_a, piece_b, trade, pass_a, pass_b):
        copy.wait_send()


def section(step_index, hist_level, feats, conv_weight, conv_bias, lat_weight, noise, hist, w_in, w_hist, gain, k_gain,
            q_gain, live, w_query, w_key, w_value, w_out):
    rows = feats.shape[0] * feats.shape[1] // 2
    width, cols = w_key.shape
    heads = cols // 128
    tall = rows * heads
    count = live.shape[1]
    chips = count // 2
    half = w_out.shape[1] // 2
    vm = pl.BlockSpec(memory_space=pltpu.VMEM)
    sm = pl.BlockSpec(memory_space=pltpu.SMEM)
    hbm = pl.BlockSpec(memory_space=pl.ANY)
    dma = pltpu.SemaphoreType.DMA
    return pl.pallas_call(
        section_kernel,
        out_shape=jax.ShapeDtypeStruct((rows, half), BF),
        in_specs=[sm, sm] + [vm] * 12 + [hbm] * 4,
        out_specs=vm,
        scratch_shapes=[
            pltpu.VMEM(feats.shape, BF),
            pltpu.VMEM(w_key.shape, BF),
            pltpu.VMEM(w_value.shape, BF),
            pltpu.VMEM((544, cols), F32),
            pltpu.VMEM((544, cols), F32),
            pltpu.VMEM((rows, width), F32),
            pltpu.VMEM((2, 128, cols), BF),
            pltpu.VMEM((64, width), BF),
            pltpu.VMEM((8, width), F32),
            pltpu.VMEM((64, 256), BF),
            pltpu.VMEM((64, 256), BF),
            pltpu.VMEM((w_out.shape[0], half), BF),
            pltpu.VMEM((w_out.shape[0], half), BF),
            pltpu.VMEM((rows, width), BF),
            pltpu.VMEM((128, 128), BF),
            pltpu.VMEM((160, width), BF),
            pltpu.VMEM((2, 128, cols), BF),
            pltpu.VMEM((2, 128, cols), BF),
            pltpu.VMEM((2, 256, cols), BF),
            pltpu.VMEM((2, 256, cols), BF),
            pltpu.VMEM((count, 128, 128), BF),
            pltpu.VMEM(w_query.shape, BF),
            pltpu.VMEM((tall, 256), BF),
            pltpu.VMEM((tall, 512), BF),
            pltpu.VMEM((256, 1536), BF),
            pltpu.VMEM((128, 1536), BF),
            pltpu.VMEM((8, 1536), F32),
            pltpu.VMEM((tall, 128), F32),
            pltpu.VMEM((tall, 128), F32),
            pltpu.VMEM((count * 8, 128), F32),
            pltpu.VMEM((count * 8, 128), F32),
            pltpu.VMEM((rows, cols), BF),
            pltpu.VMEM((rows, cols), BF),
            dma((6,)), dma((6,)), dma((6,)), dma((6,)), dma((3,)),
            dma((chips,)), dma((chips,)), dma((chips,)), dma((chips,)), dma((heads,)), dma((heads,)),
        ],
        compiler_params=pltpu.CompilerParams(collective_id=0, has_side_effects=True, vmem_limit_bytes=62 << 20),
    )(step_index, hist_level, feats, conv_weight, conv_bias, lat_weight, noise, hist, w_in, w_hist, gain, k_gain,
      q_gain, live, w_query, w_key, w_value, w_out)


def local(
    feats, conv_weight, conv_bias, latent_projection_weight, noise, step_index, hist, hist_level, hist_count,
    w_in, w_hist, norm_gain, w_query, w_key, w_value, q_gain, k_gain, w_out,
):
    return section(
        step_index, hist_level, feats.transpose(0, 2, 1), conv_weight, conv_bias[None], latent_projection_weight, noise,
        hist, w_in, w_hist.reshape(-1, w_in.shape[1]), norm_gain[None], k_gain[None], q_gain[None], hist_count[None],
        w_query, w_key, w_value, w_out)


def solution(mesh):
    placed = (
        P("seq", None, "grp"), P(), P(), P(), P("seq", None, "grp"), P(), P("seq", None), P("seq"), P(), P(), P(), P(),
        P(None, "grp"), P(None, "grp"), P(None, "grp"), P(), P(), P("grp", None),
    )
    return jax.shard_map(local, mesh=mesh, in_specs=placed, out_specs=P("seq", "grp"), check_vma=False)
```

```python
import functools
import math

import jax
import jax.numpy as jnp
from jax import lax
from jax.experimental import pallas as pl
from jax.experimental.pallas import tpu as pltpu
from jax.sharding import PartitionSpec as P

STEPS = 50
EPSILON = 1e-06
LOG2E = math.log2(math.e)
MESH = pl.DeviceIdType.MESH
BF = jnp.bfloat16
F32 = jnp.float32
LOW = -1e30


def split(x):
    hi = x.astype(BF)
    return hi, (x - hi.astype(F32)).astype(BF)


def unpack(block, kt_ref, vt_ref, c_ref):
    lane = lax.broadcasted_iota(jnp.int32, (64, 128), 1)
    lane16 = lax.broadcasted_iota(jnp.int32, (16, 128), 1)
    for pair in range(2):
        first, second = block[2 * pair].astype(F32), block[2 * pair + 1].astype(F32)

        def rest(x):
            low = x[64:96]
            return jnp.concatenate([low, pltpu.roll(low, 64, 1)], axis=0)

        tails = jnp.where(lane < 64, rest(first), pltpu.roll(rest(second), 64, 1))
        tail16 = jnp.where(lane16 < 64, first[112:128], pltpu.roll(second[112:128], 64, 1))
        parts = [
            (first[0:64], first[96:112]),
            (tails, tail16),
            (second[0:64], second[96:112]),
        ]
        for tile, (p, c16) in enumerate(parts):
            cols = slice((3 * pair + tile) * 128, (3 * pair + tile + 1) * 128)
            scales = c16[0:8] + c16[8:16]
            c_ref[:, cols] = scales
            pb = p.astype(BF)
            kt_ref[0:64, cols] = pb
            kt_ref[128:192, cols] = pb
            s_row = scales[6:7]
            vt_ref[0:64, cols] = (p * s_row).astype(BF)
            s_hi = c16[6:7]
            s_lo = c16[14:15]
            row = lax.broadcasted_iota(jnp.int32, (16, 128), 0)
            extra = jnp.where(row == 0, s_hi, jnp.where(row == 1, s_lo, jnp.where(row == 2, 1.0, 0.0)))
            vt_ref[64:80, cols] = extra.astype(BF)


NT = (((1,), (1,)), ((), ()))


def section_kernel(step_ref, level_ref, feats_ref, cw_ref, bias_ref, lw_ref, noise_ref, hist_ref, w_in_ref, wh_ref,
                   gain_ref, kg_ref, qg_ref, live_ref, wq_hbm, wk_hbm, wv_hbm, wout_hbm, out_ref,
                   early, wk, wv, acc_k, acc_v, x_ref, akc, w_perm, wave, mine, other, far_ref, near_ref,
                   tok_ref, pay_ref, lefts, akg_ref, av_ref, akh_ref, avh_ref,
                   g_ref, wq_ref, qop, qh, kt, vt, cs, acc, m_ref, hs, ax, own, theirs,
                   wk_sem, wv_sem, tsend_sem, trecv_sem, load_sem,
                   send_sem, recv_sem, fsend_sem, frecv_sem, osend_sem, orecv_sem):
    grp = lax.axis_index("grp")
    seq = lax.axis_index("seq")
    count = lax.axis_size("seq")
    core = seq % 2
    sibling = seq + 1 - 2 * core
    across = seq + 8 - 16 * ((seq // 8) % 2)
    after, before = (seq + 1) % count, (seq + count - 1) % count
    chip = seq // 2
    chips = count // 2
    frames, pixels, channels = feats_ref.shape
    rows, width = tok_ref.shape
    group = kt.shape[1] // 384
    steps = chips // group

    def shift(k):
        z = (chip // 8 + (k // 4) % 4) % 4
        x = (chip // 4 + k // 16) % 2
        y = (chip + k) % 4
        return (z * 2 + x) * 4 + y

    cols = kg_ref.shape[1] * 6
    heads = cols // 128
    chunk = 512
    quarter = far_ref.shape[0] // 4
    half = far_ref.shape[1]

    def chunk_load(source, into, sem, j):
        part = pl.ds(j * chunk, chunk)
        return pltpu.make_async_copy(source.at[part], into.at[part], sem.at[j])

    key_loads = [chunk_load(wk_hbm, wk, wk_sem, j) for j in range(width // chunk)]
    value_loads = [chunk_load(wv_hbm, wv, wv_sem, j) for j in range(width // chunk)]
    for load in key_loads + value_loads:
        load.start()

    barrier = pltpu.get_barrier_semaphore()
    for there in ((1 - grp, seq), (1 - grp, across), (grp, sibling), (grp, after), (grp, before)):
        pl.semaphore_signal(barrier, inc=1, device_id=there, device_id_type=MESH)

    plane = chips // 2

    @pl.loop(1, plane + 1)
    def _(k):
        pl.semaphore_signal(barrier, inc=1, device_id=(grp, shift(k) * 2 + core), device_id_type=MESH)

    pl.semaphore_wait(barrier, plane + 5)

    def send(n, source, into, there):
        return pltpu.make_async_remote_copy(
            src_ref=source, dst_ref=into, send_sem=tsend_sem.at[n], recv_sem=trecv_sem.at[n],
            device_id=there, device_id_type=MESH)

    halo = send(0, feats_ref, early, (grp, after))
    halo.start()
    first_rows = pl.ds(pl.multiple_of(2 * core * quarter, quarter), quarter)
    second_rows = pl.ds(pl.multiple_of((2 * core + 1) * quarter, quarter), quarter)
    far_cols = pl.ds(pl.multiple_of((1 - grp) * half, half), half)
    piece_a = send(1, wout_hbm.at[first_rows, far_cols], far_ref.at[first_rows], (1 - grp, seq))
    piece_b = send(2, wout_hbm.at[second_rows, far_cols], far_ref.at[second_rows], (1 - grp, across))

    step = step_ref[0].astype(F32)
    place = lax.broadcasted_iota(jnp.int32, (8, width), 1)
    turn = jnp.where(place < width // 2, place, place - width // 2).astype(F32)
    angle = step * jnp.exp(turn * (-math.log(10000.0) / (width // 2)))
    wave[...] = jnp.where(place < width // 2, jnp.cos(angle), jnp.sin(angle))
    lane = lax.broadcasted_iota(jnp.int32, (16, 128), 1)
    line = lax.broadcasted_iota(jnp.int32, (16, 128), 0)
    level = jnp.zeros((16, 128), F32)
    for r in range(8):
        level = jnp.where(line == r, level_ref[r].astype(F32), level)
    base = jnp.concatenate([hist_ref[...].astype(F32), jnp.zeros((8, 64), F32)], axis=1)
    base = jnp.concatenate([base, jnp.zeros((8, 128), F32)], axis=0)
    moved = pltpu.roll(base, 64, 1)
    spread = jnp.concatenate([
        jnp.where(level == jnp.where(lane < 64, 0.0, 1.0), base + moved, 0.0),
        jnp.where(level == 2.0, base, 0.0)], axis=1).astype(BF)
    r64 = lax.broadcasted_iota(jnp.int32, (64, 64), 0)
    c64 = lax.broadcasted_iota(jnp.int32, (64, 64), 1)
    order = jnp.where(c64 == (r64 % 16) * 4 + r64 // 16, 1.0, 0.0).astype(BF)

    square = jnp.zeros((16, 1), F32)
    for j in range(width // chunk):
        part = slice(j * chunk, (j + 1) * chunk)
        gain = gain_ref[:, part]
        low = jnp.dot(order, w_in_ref[:, part], preferred_element_type=F32)
        w_perm[:, part] = low.astype(BF)
        low_hi, low_lo = split(low * gain)
        e_hi, e_lo = split(jnp.concatenate([wave[:, part]] * 2, axis=0) * gain)
        raw = jnp.dot(spread[:, :192], wh_ref[:, part], preferred_element_type=F32)
        square = square + jnp.sum(raw * raw, axis=1, keepdims=True)
        r_hi, r_lo = split(raw * gain)
        base_rows = jnp.concatenate([low_hi, low_lo, e_hi, e_lo], axis=0)
        lefts[:, part] = base_rows
        key_loads[j].wait()
        k = jnp.dot(jnp.concatenate([base_rows, r_hi, r_lo], axis=0), wk[part, :], preferred_element_type=F32)
        acc_k[0:192, :] = k if j == 0 else acc_k[0:192, :] + k

    def put(ref, full):
        hi, lo = split(full)
        ref[0] = hi
        ref[1] = lo

    def low_parts(acc):
        a = acc[0:64, :] + acc[64:128, :]
        b = acc[128:144, :] + acc[144:160, :]
        return a, b, lax.broadcasted_iota(jnp.int32, b.shape, 0)

    kg = jnp.concatenate([kg_ref[...]] * heads, axis=1)
    pad = jnp.zeros((48, cols), F32)
    a, b, row = low_parts(acc_k)
    full = jnp.concatenate([a, jnp.where(row == 0, b, 0.0), pad], axis=0)
    put(akc, full)
    put(akg_ref, full * kg)
    y = acc_k[160:176, :] + acc_k[176:192, :]
    s = lax.rsqrt(jnp.broadcast_to(square, (16, 128)) * (1.0 / width) + EPSILON)
    wide = jnp.where(lane == 70, s, 0.0)
    for head in range(heads):
        part = y[:, head * 128:(head + 1) * 128]
        mean = jnp.mean(part * part, axis=1, keepdims=True)
        wide = jnp.where(lane == 64 + head, s * lax.rsqrt(s * s * mean + EPSILON) * (LOG2E / math.sqrt(128.0)), wide)
    hi = wide.astype(BF).astype(F32)
    aux = jnp.where(lane == 80, level, hi + pltpu.roll(wide - hi, 8, 1))
    owner = lax.broadcasted_iota(jnp.int32, live_ref.shape, 1)
    live = jnp.sum(jnp.where(owner == seq, live_ref[...].astype(F32), 0.0), axis=1, keepdims=True)
    aux = jnp.where(lane == 81, jnp.where(line.astype(F32) < live, 1.0, 0.0), aux)
    slots = jnp.concatenate([moved[0:8], aux[0:8]], axis=0)

    load_query = pltpu.make_async_copy(wq_hbm, wq_ref, load_sem.at[0])
    load_query.start()
    near_cols = pl.ds(pl.multiple_of(grp * half, half), half)
    load_near = pltpu.make_async_copy(wout_hbm.at[:, near_cols], near_ref, load_sem.at[1])
    load_near.start()
    sigma = (STEPS - step) / STEPS
    bias = jnp.transpose(jnp.broadcast_to(bias_ref[...], (128, 128)))[:, 0:1]
    halo.wait_recv()
    lead = jnp.where(seq > 0, 1.0, 0.0)
    window = [jnp.where(lead > 0.5, early[0], jnp.zeros_like(early[0])),
              jnp.where(lead > 0.5, early[1], jnp.zeros_like(early[1])), feats_ref[0], feats_ref[1]]
    pixel = lax.broadcasted_iota(jnp.int32, (pixels, 256), 0)
    col = lax.broadcasted_iota(jnp.int32, (pixels, 256), 1)
    lines = [jnp.zeros((lw_ref.shape[0], 256), F32) for _ in range(4)]
    for t in range(frames):
        total = jnp.zeros((channels, pixels), F32)
        for tap in range(3):
            total = total + lax.dot_general(cw_ref[tap], window[2 + t - tap], NT, preferred_element_type=F32)
        total = total + bias
        hidden = (total * (1.0 / (1.0 + jnp.exp(-total)))).astype(BF)
        latent = jnp.dot(lw_ref[...], hidden, preferred_element_type=F32)
        noisy = ((1.0 - sigma) * latent + sigma * noise_ref[t].astype(F32)).astype(BF)
        for i in range(4):
            hit = (pixel % 4 == i) & (col == t * (pixels // 2) + grp * (pixels // 4) + pixel // 4)
            lines[i] = lines[i] + jnp.dot(noisy, jnp.where(hit, 1.0, 0.0).astype(BF), preferred_element_type=F32)
    mine[...] = jnp.concatenate(lines, axis=0).astype(BF)
    trade = send(3, mine, other, (1 - grp, seq))
    trade.start()
    pass_a = send(4, far_ref.at[first_rows], far_ref.at[first_rows], (grp, sibling))
    pass_b = send(5, far_ref.at[second_rows], far_ref.at[second_rows], (grp, sibling))
    trade.wait_recv()

    pt = mine[...].astype(F32) + other[...].astype(F32)
    row = lax.broadcasted_iota(jnp.int32, (64, 256), 0)
    tall = jnp.concatenate([pt, jnp.where(row == 0, 1.0, 0.0)], axis=0)
    px = jnp.transpose(tall)[:rows].astype(BF)
    p = px[:, :64]
    total = jnp.zeros((rows, 1), F32)
    total_row = jnp.zeros((8, rows), F32)
    ones = jnp.ones((8, chunk), BF)
    for j in range(width // chunk):
        part = slice(j * chunk, (j + 1) * chunk)
        x = jnp.dot(p, w_perm[:, part], preferred_element_type=F32) + wave[0:1, part]
        x_ref[:, part] = x
        x2 = x * x
        total = total + jnp.sum(x2, axis=1, keepdims=True)
        hi, lo = split(x2)
        total_row = total_row + lax.dot_general(ones, hi, NT, preferred_element_type=F32)
        total_row = total_row + lax.dot_general(ones, lo, NT, preferred_element_type=F32)
    s = lax.rsqrt(total * (1.0 / width) + EPSILON)
    s_row = lax.rsqrt(total_row * (1.0 / width) + EPSILON)
    y = jnp.dot(px, akc[0], preferred_element_type=F32) + jnp.dot(px, akc[1], preferred_element_type=F32)
    hi, lo = split(y * y)
    r8 = lax.broadcasted_iota(jnp.int32, (8, cols), 0)
    c8 = lax.broadcasted_iota(jnp.int32, (8, cols), 1)
    pick = jnp.where(c8 // 128 == r8, 1.0, 0.0).astype(BF)
    mean = (lax.dot_general(pick, hi, NT, preferred_element_type=F32)
            + lax.dot_general(pick, lo, NT, preferred_element_type=F32)) * (1.0 / 128)
    c = s_row * lax.rsqrt(s_row * s_row * mean + EPSILON) * (LOG2E / math.sqrt(128.0))
    r = lax.broadcasted_iota(jnp.int32, (8, rows), 0)
    both = jnp.where(r < heads, c, jnp.where(r == 6, s_row, 0.0))
    both = jnp.concatenate([both, jnp.zeros((8, 256 - rows), F32)], axis=1)
    hi8 = both.astype(BF).astype(F32)
    c16 = jnp.concatenate([hi8, both - hi8], axis=0)
    pay_ref[0:64, :] = pt[:, 0:128].astype(BF)
    lane32 = lax.broadcasted_iota(jnp.int32, (32, 128), 1)
    pay_ref[64:96, :] = jnp.where(lane32 < 64, pt[0:32, 128:256], pltpu.roll(pt[32:64, 128:256], 64, 1)).astype(BF)
    pay_ref[96:112, :] = c16[:, 0:128].astype(BF)
    pay_ref[112:128, :] = (c16[:, 128:256] + slots).astype(BF)
    def direct(k):
        return pltpu.make_async_remote_copy(
            src_ref=pay_ref, dst_ref=g_ref.at[core, k], send_sem=send_sem.at[k], recv_sem=recv_sem.at[k],
            device_id=(grp, shift(k) * 2 + core), device_id_type=MESH)

    def forward(n):
        lot = g_ref.at[core, pl.ds(n * group, group)]
        return pltpu.make_async_remote_copy(
            src_ref=lot, dst_ref=lot, send_sem=fsend_sem.at[n], recv_sem=frecv_sem.at[n],
            device_id=(grp, sibling), device_id_type=MESH)

    def relay(k):
        return pltpu.make_async_remote_copy(
            src_ref=g_ref.at[core, plane], dst_ref=g_ref.at[core, k], send_sem=send_sem.at[k], recv_sem=recv_sem.at[k],
            device_id=(grp, shift(k - plane) * 2 + core), device_id_type=MESH)

    direct(plane).start()

    @pl.loop(1, plane)
    def _(k):
        direct(k).start()

    here = pltpu.make_async_copy(pay_ref, g_ref.at[core, 0], load_sem.at[2])
    here.start()
    here.wait()

    for j in range(width // chunk):
        part = slice(j * chunk, (j + 1) * chunk)
        tok_ref[:, part] = (x_ref[:, part] * s * gain_ref[:, part]).astype(BF)

    one_row = lax.broadcasted_iota(jnp.int32, (64, kt.shape[1]), 0)
    ones = jnp.where(one_row == 0, 1.0, 0.0).astype(BF)
    kt[64:128, :] = ones
    kt[192:256, :] = ones
    vt[80:128, :] = jnp.zeros((48, vt.shape[1]), BF)
    acc[...] = jnp.zeros_like(acc)
    m_ref[...] = jnp.full(m_ref.shape, LOW, F32)
    direct(plane).wait_recv()

    @pl.loop(plane + 1, chips)
    def _(k):
        relay(k).start()

    for j in range(width // chunk):
        part = slice(j * chunk, (j + 1) * chunk)
        h_hi, h_lo = split(wh_ref[:, part].astype(F32) * gain_ref[:, part])
        both_h = jnp.concatenate([h_hi, h_lo], axis=0)
        k = jnp.dot(both_h, wk[part, :], preferred_element_type=F32)
        value_loads[j].wait()
        v = jnp.dot(jnp.concatenate([lefts[:, part], both_h], axis=0), wv[part, :], preferred_element_type=F32)
        acc_k[0:384, :] = k if j == 0 else acc_k[0:384, :] + k
        acc_v[...] = v if j == 0 else acc_v[...] + v
    pad_h = jnp.zeros((64, cols), F32)
    put(akh_ref, jnp.concatenate([acc_k[0:192, :] + acc_k[192:384, :], pad_h], axis=0) * kg)
    a, b, row = low_parts(acc_v)
    put(av_ref, jnp.concatenate([a, jnp.where(row < 2, b, 0.0), pad], axis=0))
    put(avh_ref, jnp.concatenate([acc_v[160:352, :] + acc_v[352:544, :], pad_h], axis=0))

    @pl.loop(1, group)
    def _(k):
        direct(k).wait_recv()

    forward(0).start()

    load_query.wait()
    for h in range(heads):
        sl = slice(h * rows, (h + 1) * rows)
        cols = slice(h * 128, (h + 1) * 128)
        q = jnp.dot(tok_ref[...], wq_ref[:, cols], preferred_element_type=F32)
        q = (q * lax.rsqrt(jnp.mean(q * q, axis=1, keepdims=True) + EPSILON) * qg_ref[...]).astype(BF)
        for ref, a_ref, n in ((qop, akg_ref, 128), (qh, akh_ref, 256)):
            qp = (lax.dot_general(q, a_ref[0, :, cols], NT, preferred_element_type=F32)
                  + lax.dot_general(q, a_ref[1, :, cols], NT, preferred_element_type=F32))
            hi, lo = split(qp)
            ref[sl, 0:n] = hi
            ref[sl, n:2 * n] = lo

    @pl.loop(group, 2 * group)
    def _(k):
        direct(k).wait_recv()

    forward(1).start()

    def absorb(h, s):
        sl = slice(h * rows, (h + 1) * rows)
        old = m_ref[sl, :]
        tiles = [s[:, j * 128:(j + 1) * 128] for j in range(s.shape[1] // 128)]
        top = functools.reduce(jnp.maximum, tiles)
        new = jnp.maximum(old, jnp.broadcast_to(jnp.max(top, axis=1, keepdims=True), old.shape))
        w = jnp.concatenate([jnp.exp2(t - new).astype(BF) for t in tiles], axis=1)
        m_ref[sl, :] = new
        return w, jnp.exp2(old - new)

    def take(i):
        forward(i).wait_recv()
        for b in range(0, group, 2):
            lot = slice(b * 384, b * 384 + 768)
            k = group * i + b
            unpack([g_ref[0, k], g_ref[1, k], g_ref[0, k + 1], g_ref[1, k + 1]],
                   kt.at[:, lot], vt.at[:, lot], cs.at[:, lot])

    def scores(h):
        return jnp.dot(qop[h * rows:(h + 1) * rows, :], kt[...], preferred_element_type=F32)

    @pl.loop(0, steps - 1)
    def _(i):
        take(i)

        def some(first, last):
            ahead = scores(first)
            for h in range(first, last):
                s = ahead
                if h + 1 < last:
                    ahead = scores(h + 1)
                sl = slice(h * rows, (h + 1) * rows)
                w, keep = absorb(h, s * cs[h:h + 1, :])
                acc[sl, :] = acc[sl, :] * keep + lax.dot_general(w, vt[...], NT, preferred_element_type=F32)

        some(0, heads // 2)

        @pl.when((i + 2 < steps) & (i + 2 != steps // 2))
        def _():
            for b in range(group):
                direct(group * (i + 2) + b).wait_recv()
            forward(i + 2).start()

        @pl.when(i + 2 == steps // 2)
        def _():
            for b in range(1, group):
                direct(plane + b).wait_recv()
            forward(i + 2).start()

        @pl.when(i == 0)
        def _():
            piece_a.start()
            piece_b.start()

        @pl.when(i == steps - 2)
        def _():
            piece_a.wait_recv()
            pass_a.start()
            piece_b.wait_recv()
            pass_b.start()

        some(heads // 2, heads)

    take(steps - 1)

    @pl.loop(0, chips // 4)
    def _(n):
        for b in range(8):
            piece = pltpu.roll(g_ref[n // 4, (n % 4) * 8 + b, 112:128, :].astype(F32), 64, 1)
            spot = pl.ds(pl.multiple_of(n * 64 + b * 8, 8), 8)
            hs[spot, :] = piece[0:8]
            ax[spot, :] = piece[8:16]

    lane = lax.broadcasted_iota(jnp.int32, hs.shape, 1)
    level = ax[:, 16:17]
    size = ax[:, 6:7] + ax[:, 14:15]
    base = jnp.where(lane < 64, hs[...], 0.0)
    twice = base + pltpu.roll(base, 64, 1)
    first = jnp.where(level == jnp.where(lane < 64, 0.0, 1.0), twice, 0.0)
    second = jnp.where(level == 2.0, base, 0.0)
    kh = jnp.concatenate([first, second], axis=1).astype(BF)
    vh = jnp.concatenate([first * size, jnp.where(lane == 64, 1.0, second * size)], axis=1).astype(BF)
    across = jnp.transpose(ax[...])
    ch = across[0:8] + across[8:16]
    hbias = jnp.where(across[17:18] > 0.5, 0.0, LOW)

    def hist_scores(h):
        sl = slice(h * rows, (h + 1) * rows)
        return (lax.dot_general(qh[sl, 0:256], kh, NT, preferred_element_type=F32)
                + lax.dot_general(qh[sl, 256:512], kh, NT, preferred_element_type=F32))

    def share(h):
        lot = slice(h * 128, (h + 1) * 128)
        return pltpu.make_async_remote_copy(
            src_ref=own.at[:, lot], dst_ref=theirs.at[:, lot], send_sem=osend_sem.at[h],
            recv_sem=orecv_sem.at[h], device_id=(1 - grp, seq), device_id_type=MESH)

    def both_scores(h):
        return scores(h), hist_scores(h)

    ahead = both_scores(0)
    for h in range(heads):
        s, t = ahead
        if h + 1 < heads:
            ahead = both_scores(h + 1)
        sl = slice(h * rows, (h + 1) * rows)
        lot = slice(h * 128, (h + 1) * 128)
        wide_s = jnp.concatenate([s * cs[h:h + 1, :], t * ch[h:h + 1, :] + hbias], axis=1)
        w, keep = absorb(h, wide_s)
        n = s.shape[1]
        a = acc[sl, :] * keep + lax.dot_general(w[:, :n], vt[...], NT, preferred_element_type=F32)
        b = jnp.dot(w[:, n:], vh, preferred_element_type=F32)
        if h > 0:
            share(h - 1).start()
        o = jnp.zeros((rows, 128), F32)
        for value, weight in ((a, av_ref), (b, avh_ref)):
            hi, lo = split(value)
            o = o + jnp.dot(hi, weight[0, :, lot], preferred_element_type=F32)
            o = o + jnp.dot(lo, weight[0, :, lot], preferred_element_type=F32)
            o = o + jnp.dot(hi, weight[1, :, lot], preferred_element_type=F32)
        own[:, lot] = (o / (a[:, 66:67] + b[:, 192:193])).astype(BF)
    share(heads - 1).start()

    load_near.wait()
    for j in range(half // chunk):
        part = slice(j * chunk, (j + 1) * chunk)
        x_ref[:, part] = jnp.dot(own[...], near_ref[:, part], preferred_element_type=F32)
    pass_a.wait_recv()
    pass_b.wait_recv()
    for h in range(heads):
        share(h).wait_recv()
    for j in range(half // chunk):
        part = slice(j * chunk, (j + 1) * chunk)
        out_ref[:, part] = (x_ref[:, part]
                            + jnp.dot(theirs[...], far_ref[:, part], preferred_element_type=F32)).astype(BF)

    @pl.loop(0, steps)
    def _(n):
        forward(n).wait_send()

    @pl.loop(1, plane + 1)
    def _(k):
        direct(k).wait_send()

    @pl.loop(plane + 1, chips)
    def _(k):
        relay(k).wait_send()

    for h in range(heads):
        share(h).wait_send()
    for copy in (halo, piece_a, piece_b, trade, pass_a, pass_b):
        copy.wait_send()


def section(step_index, hist_level, feats, conv_weight, conv_bias, lat_weight, noise, hist, w_in, w_hist, gain, k_gain,
            q_gain, live, w_query, w_key, w_value, w_out):
    rows = feats.shape[0] * feats.shape[1] // 2
    width, cols = w_key.shape
    heads = cols // 128
    tall = rows * heads
    count = live.shape[1]
    chips = count // 2
    half = w_out.shape[1] // 2
    vm = pl.BlockSpec(memory_space=pltpu.VMEM)
    sm = pl.BlockSpec(memory_space=pltpu.SMEM)
    hbm = pl.BlockSpec(memory_space=pl.ANY)
    dma = pltpu.SemaphoreType.DMA
    return pl.pallas_call(
        section_kernel,
        out_shape=jax.ShapeDtypeStruct((rows, half), BF),
        in_specs=[sm, sm] + [vm] * 12 + [hbm] * 4,
        out_specs=vm,
        scratch_shapes=[
            pltpu.VMEM(feats.shape, BF),
            pltpu.VMEM(w_key.shape, BF),
            pltpu.VMEM(w_value.shape, BF),
            pltpu.VMEM((544, cols), F32),
            pltpu.VMEM((544, cols), F32),
            pltpu.VMEM((rows, width), F32),
            pltpu.VMEM((2, 128, cols), BF),
            pltpu.VMEM((64, width), BF),
            pltpu.VMEM((8, width), F32),
            pltpu.VMEM((64, 256), BF),
            pltpu.VMEM((64, 256), BF),
            pltpu.VMEM((w_out.shape[0], half), BF),
            pltpu.VMEM((w_out.shape[0], half), BF),
            pltpu.VMEM((rows, width), BF),
            pltpu.VMEM((128, 128), BF),
            pltpu.VMEM((160, width), BF),
            pltpu.VMEM((2, 128, cols), BF),
            pltpu.VMEM((2, 128, cols), BF),
            pltpu.VMEM((2, 256, cols), BF),
            pltpu.VMEM((2, 256, cols), BF),
            pltpu.VMEM((2, chips, 128, 128), BF),
            pltpu.VMEM(w_query.shape, BF),
            pltpu.VMEM((tall, 256), BF),
            pltpu.VMEM((tall, 512), BF),
            pltpu.VMEM((256, 1536), BF),
            pltpu.VMEM((128, 1536), BF),
            pltpu.VMEM((8, 1536), F32),
            pltpu.VMEM((tall, 128), F32),
            pltpu.VMEM((tall, 128), F32),
            pltpu.VMEM((count * 8, 128), F32),
            pltpu.VMEM((count * 8, 128), F32),
            pltpu.VMEM((rows, cols), BF),
            pltpu.VMEM((rows, cols), BF),
            dma((6,)), dma((6,)), dma((6,)), dma((6,)), dma((3,)),
            dma((chips,)), dma((chips,)), dma((chips,)), dma((chips,)), dma((heads,)), dma((heads,)),
        ],
        compiler_params=pltpu.CompilerParams(collective_id=0, has_side_effects=True, vmem_limit_bytes=62 << 20),
    )(step_index, hist_level, feats, conv_weight, conv_bias, lat_weight, noise, hist, w_in, w_hist, gain, k_gain,
      q_gain, live, w_query, w_key, w_value, w_out)


def local(
    feats, conv_weight, conv_bias, latent_projection_weight, noise, step_index, hist, hist_level, hist_count,
    w_in, w_hist, norm_gain, w_query, w_key, w_value, q_gain, k_gain, w_out,
):
    return section(
        step_index, hist_level, feats.transpose(0, 2, 1), conv_weight, conv_bias[None], latent_projection_weight, noise,
        hist, w_in, w_hist.reshape(-1, w_in.shape[1]), norm_gain[None], k_gain[None], q_gain[None], hist_count[None],
        w_query, w_key, w_value, w_out)


def solution(mesh):
    placed = (
        P("seq", None, "grp"), P(), P(), P(), P("seq", None, "grp"), P(), P("seq", None), P("seq"), P(), P(), P(), P(),
        P(None, "grp"), P(None, "grp"), P(None, "grp"), P(), P(), P("grp", None),
    )
    return jax.shard_map(local, mesh=mesh, in_specs=placed, out_specs=P("seq", "grp"), check_vma=False)
```
